32 devices in a mesh: groups: 2 (over y), seq: 4 (over z), head: 2 (over x), batch: 2 (over core).
Axes of the slice: x: 2, y: 2, z: 4, core: 2. Of those that a mesh axis runs over, the one named last changes fastest.
Arguments:
- hidden_in: bfloat16 [4, 1024, 8192], P(('groups', 'batch'), 'seq', 'head'), parts along dimension 0, may hold values from -6 to 6
- teacher_query: bfloat16 [4, 1024, 4096], P(('groups', 'batch'), 'seq', 'head'), parts along dimension 0, may hold values from -48 to 48
- teacher_key: bfloat16 [4, 1024, 512], P(('groups', 'batch'), 'seq'), parts along dimension 0, may hold values from -6 to 6
- proj_c: bfloat16 [8192, 4096], P('seq', 'head'), may hold values from -0.00390625 to 0.00390625
- proj_b: bfloat16 [8192, 512], P('seq'), may hold values from -0.0029296875 to 0.0029296875
- proj_step: bfloat16 [8192, 32], P('seq', 'head'), may hold values from -0.0625 to 0.0625
- decay_rate: float32 [32], P('head'), may hold values from 0.0001 to 0.06
Outputs:
- row_loss: float32 [4, 32, 1024], P(('groups', 'batch'), 'head', 'seq'), parts along dimension 0
The draws below stay inside these ranges and needn't reach their ends.
There are 2 independent parts, one for each index of `groups`. The reference program is written for one: setup_inputs(seed, part) draws one part's arguments, and reference() takes and returns one part's arrays. A program takes and returns all parts, laid end to end along the dimension named above; an argument that names none is the same for every part. Nothing has to cross between parts.
All inputs are finite; a program needn't handle non-finite values.
Results may differ from the reference program's by a relative error of at most 0.0015.
Values may be sent and summed in bfloat16 or wider, within the bound.
No kernel may reach another device: no remote copies, remote signals or barrier semaphores. Data moves between devices by JAX's collectives and lax.ppermute only.
A program may use at most 128 MiB of HBM per device.

```python
import math
import jax
import jax.numpy as jnp
from jax import lax

D = 8192
HEADS = 32
KV_HEADS = 4
HEAD_DIM = 128
LENGTH = 1024
SEQS = 2


def teacher_pair(key):
    per_group = HEADS // KV_HEADS
    key_keys = jax.random.fold_in(key, 11)
    key_query = jax.random.fold_in(key, 12)
    keys_drawn = jnp.clip(jax.random.normal(key_keys, (SEQS, LENGTH, KV_HEADS, HEAD_DIM), jnp.float32), -6.0, 6.0)
    query_drawn = jnp.clip(3.0 * jax.random.normal(key_query, (SEQS, LENGTH, KV_HEADS, per_group, HEAD_DIM), jnp.float32), -48.0, 48.0)
    return (query_drawn.reshape(SEQS, LENGTH, HEADS * HEAD_DIM), keys_drawn.reshape(SEQS, LENGTH, KV_HEADS * HEAD_DIM))


def draw_teacher_query(key, part):
    return teacher_pair(key)[0].astype(jnp.bfloat16)


def draw_teacher_key(key, part):
    return teacher_pair(key)[1].astype(jnp.bfloat16)


def levels(key, extent, pieces, least, top_value):
    def one(position, blocks):
        heights = jax.random.uniform(jax.random.fold_in(jax.random.fold_in(key, 6), position), (blocks,), jnp.float32, least / len(pieces), top_value / len(pieces))
        return jnp.repeat(jnp.exp(heights), extent[position] // blocks).reshape((-1,) + (1,) * (len(extent) - position - 1))

    gain = one(*pieces[0])
    for cut in pieces[1:]:
        gain = gain * one(*cut)
    return gain


def centred(own_key, extent, width, limit, pieces=(), held_as=jnp.bfloat16):
    drawn = width * jax.random.normal(own_key, extent, jnp.float32)
    if pieces:
        drawn = drawn * levels(own_key, extent, pieces, -0.22, 0.18)
    return jnp.clip(drawn, -limit, limit).astype(held_as)


def setup_inputs(seed: int = 0, part: int = 0) -> dict:
    arg_keys = jax.random.split(jax.random.key(seed), 8)
    own_keys = jax.random.split(jax.random.fold_in(arg_keys[7], part), 8)
    return {
        "hidden_in": centred(own_keys[0], (SEQS, LENGTH, D), 1.0, 6.0, ((0, 2), (1, 4), (2, 2))),
        "teacher_query": draw_teacher_query(jax.random.fold_in(jax.random.fold_in(arg_keys[7], part), 71), part),
        "teacher_key": draw_teacher_key(jax.random.fold_in(jax.random.fold_in(arg_keys[7], part), 71), part),
        "proj_c": centred(arg_keys[3], (D, HEADS * HEAD_DIM), (2 * D * HEAD_DIM) ** -0.5, 0.00390625, ((0, 4), (1, 2))),
        "proj_b": centred(arg_keys[4], (D, KV_HEADS * HEAD_DIM), (D * LENGTH // 2) ** -0.5, 0.0029296875, ((0, 4),)),
        "proj_step": centred(arg_keys[5], (D, HEADS), D ** -0.5, 0.0625, ((0, 4), (1, 2))),
        "decay_rate": jnp.clip(jnp.exp(math.log(0.06) - 6.3969297 * jax.random.uniform(arg_keys[6], (HEADS,), jnp.float32) ** levels(arg_keys[6], (HEADS,), ((0, 2),), -0.2, 0.2)), 0.0001, 0.06),
    }


def reference(hidden_in, teacher_query, teacher_key, proj_c, proj_b, proj_step, decay_rate):
    per_group = HEADS // KV_HEADS
    token_rows = hidden_in.reshape(SEQS * LENGTH, D)
    readout = jnp.dot(token_rows, proj_c, preferred_element_type=jnp.float32).astype(jnp.bfloat16)
    inputs = jnp.dot(token_rows, proj_b, preferred_element_type=jnp.float32).astype(jnp.bfloat16)
    step_size = jax.nn.softplus(jnp.dot(token_rows, proj_step, preferred_element_type=jnp.float32))
    step_size = step_size.reshape(SEQS, LENGTH, HEADS)
    cumulated = jnp.cumsum(-decay_rate[None, None, :] * step_size, axis=1)
    query_t = teacher_query.reshape(SEQS, LENGTH, KV_HEADS, per_group, HEAD_DIM)
    query_c = readout.reshape(SEQS, LENGTH, KV_HEADS, per_group, HEAD_DIM)
    keys_t = teacher_key.reshape(SEQS, LENGTH, KV_HEADS, HEAD_DIM)
    keys_b = inputs.reshape(SEQS, LENGTH, KV_HEADS, HEAD_DIM)
    steps_g = step_size.reshape(SEQS, LENGTH, KV_HEADS, per_group)
    cum_g = cumulated.reshape(SEQS, LENGTH, KV_HEADS, per_group)
    query_block = min(512, LENGTH)
    block_count = LENGTH // query_block
    key_pos = jnp.arange(LENGTH, dtype=jnp.int32)

    def one_item(item):
        seq_index = (item // (KV_HEADS * block_count)).astype(jnp.int32)
        group_index = ((item // block_count) % KV_HEADS).astype(jnp.int32)
        row_start = ((item % block_count) * query_block).astype(jnp.int32)
        zero_index = jnp.zeros((), jnp.int32)
        query_here = lax.dynamic_slice(query_t, (seq_index, row_start, group_index, zero_index, zero_index), (1, query_block, 1, per_group, HEAD_DIM))[0, :, 0].astype(jnp.float32)
        readout_here = lax.dynamic_slice(query_c, (seq_index, row_start, group_index, zero_index, zero_index), (1, query_block, 1, per_group, HEAD_DIM))[0, :, 0].astype(jnp.float32)
        key_here = lax.dynamic_slice(keys_t, (seq_index, zero_index, group_index, zero_index), (1, LENGTH, 1, HEAD_DIM))[0, :, 0].astype(jnp.float32)
        input_here = lax.dynamic_slice(keys_b, (seq_index, zero_index, group_index, zero_index), (1, LENGTH, 1, HEAD_DIM))[0, :, 0].astype(jnp.float32)
        steps_here = lax.dynamic_slice(steps_g, (seq_index, zero_index, group_index, zero_index), (1, LENGTH, 1, per_group))[0, :, 0]
        cum_keys = lax.dynamic_slice(cum_g, (seq_index, zero_index, group_index, zero_index), (1, LENGTH, 1, per_group))[0, :, 0]
        cum_query = lax.dynamic_slice(cum_g, (seq_index, row_start, group_index, zero_index), (1, query_block, 1, per_group))[0, :, 0]
        scores = jnp.einsum("qpn,kn->pqk", query_here, key_here) * HEAD_DIM ** -0.5
        query_pos = row_start + jnp.arange(query_block, dtype=jnp.int32)
        allowed = key_pos[None, :] <= query_pos[:, None]
        masked = jnp.where(allowed, scores, -jnp.inf)
        probs = jnp.exp(masked - jnp.max(masked, axis=-1, keepdims=True))
        probs = probs / jnp.sum(probs, axis=-1, keepdims=True)
        inner_prod = jnp.einsum("qpn,kn->pqk", readout_here, input_here)
        log_gap = jnp.where(allowed, jnp.transpose(cum_query)[:, :, None] - jnp.transpose(cum_keys)[:, None, :], -jnp.inf)
        mixer_tile = inner_prod * jnp.transpose(steps_here)[:, None, :] * jnp.exp(log_gap)
        return jnp.sum((probs - mixer_tile) ** 2, axis=-1)

    losses = lax.map(one_item, jnp.arange(SEQS * KV_HEADS * block_count, dtype=jnp.int32))
    losses = losses.reshape(SEQS, KV_HEADS, block_count, per_group, query_block)
    return jnp.transpose(losses, (0, 1, 3, 2, 4)).reshape(SEQS, HEADS, LENGTH)
```

```python
import functools
import math

import jax
import jax.numpy as jnp
from jax import lax
from jax.experimental import pallas as pl
from jax.experimental.pallas import tpu as pltpu
from jax.sharding import PartitionSpec as P

HEADS = 32
KV_HEADS = 4
HEAD_DIM = 128
LOG2E = math.log2(math.e)
BF16 = jnp.bfloat16
F32 = jnp.float32
VMEM_LIMIT = 48 * 1024 * 1024

NT = (((1,), (1,)), ((), ()))


def xor_permute(value, axis, offset):
    size = lax.axis_size(axis)
    return lax.ppermute(value, axis, [(i, i ^ offset) for i in range(size)])


def whole(shape):
    return pl.BlockSpec(shape, lambda *_: (0,) * len(shape))


def columns(rows, width, index):
    return pl.BlockSpec((rows, width), lambda *_: (0, index))


def smem():
    return pl.BlockSpec(memory_space=pltpu.SMEM)


def call(kernel, args, in_specs, out_shapes, name, scratch=()):
    return pl.pallas_call(
        kernel,
        grid=(1,),
        in_specs=in_specs,
        out_specs=tuple(whole(s.shape) for s in out_shapes),
        out_shape=tuple(out_shapes),
        scratch_shapes=list(scratch),
        compiler_params=pltpu.CompilerParams(vmem_limit_bytes=VMEM_LIMIT),
        name=name,
    )(*args)


def product(place, act, own, pieces, model):
    block, quarter = place[0], place[1]
    rows = own.shape[0]
    total = jnp.dot(
        act[:, pl.ds(pl.multiple_of(block * rows, rows), rows)], own[...], preferred_element_type=F32
    )
    for piece, (step, turn) in zip(pieces, model):
        part = piece.shape[0]
        start = (block ^ step) * rows + (quarter ^ turn) * part
        total += jnp.dot(
            act[:, pl.ds(pl.multiple_of(start, part), part)], piece[...], preferred_element_type=F32
        )
    return total


def partial_kernel(model, place, act, own, *rest):
    pieces, out = rest[:-1], rest[-1]
    out[...] = product(place, act, own, pieces, model).astype(out.dtype)


def extra_kernel(model, step_model, place, act_own, act_other, own, *rest):
    n = len(model)
    pieces = rest[:n]
    step_pieces = rest[n : n + len(step_model)]
    full, rounded, raw = rest[-3:]
    tokens = act_own.shape[0]
    for at, act in enumerate((act_own, act_other)):
        here = slice(at * tokens, (at + 1) * tokens)
        value = product(place, act, own, pieces, model)
        full[here, :] = value
        rounded[here, :] = value.astype(BF16)
        total = None
        for piece, step in zip(step_pieces, step_model):
            rows = piece.shape[1]
            start = pl.multiple_of((place[0] ^ step) * rows, rows)
            part = lax.dot_general(piece[...], act[:, pl.ds(start, rows)], NT, preferred_element_type=F32)
            total = part if total is None else total + part
        raw[:, here] = total


def decay_kernel(offsets, place, raw, rate, factor, log_row, log_col, gain_col):
    mine = place[2]
    heads, tokens = raw.shape[1], raw.shape[2]
    lane = lax.broadcasted_iota(jnp.int32, (heads, tokens), 1)
    steps, logs, totals = [], [], []
    for at in range(len(offsets)):
        value = raw[at]
        step = jnp.maximum(value, 0.0) + jnp.log1p(jnp.exp(-jnp.abs(value)))
        log = step * (-LOG2E * rate[...])
        shift = 1
        while shift < tokens:
            log = log + jnp.where(lane >= shift, pltpu.roll(log, shift, 1), 0.0)
            shift *= 2
        steps.append(step)
        logs.append(log)
        totals.append(log[:, tokens - 1 :])
    for at, offset in enumerate(offsets):
        here = slice(at * tokens, (at + 1) * tokens)
        if at == 0:
            factor[:, here] = steps[0]
            continue
        between = jnp.zeros_like(totals[0])
        first = mine ^ offset
        for other, distance in enumerate(offsets):
            block = mine ^ distance
            inside = jnp.logical_and(block > first, block < mine)
            between += jnp.where(inside, totals[other], 0.0)
        factor[:, here] = steps[at] * jnp.exp2(totals[at] - logs[at] + between)
    log_row[...] = logs[0]
    wide = jnp.concatenate([logs[0], jnp.zeros((128 - heads, tokens), F32)], axis=0)
    turned = wide.T
    log_col[...] = turned
    gain_col[...] = jnp.exp2(turned)


def causal_of(tokens):
    row = lax.broadcasted_iota(jnp.int32, (tokens, tokens), 0)
    col = lax.broadcasted_iota(jnp.int32, (tokens, tokens), 1)
    return col <= row


def folded(combine, value):
    parts = [value[:, i : i + 128] for i in range(0, value.shape[1], 128)]
    return functools.reduce(combine, parts)


SCALE = LOG2E * HEAD_DIM ** -0.5


def teacher_kernel(offsets, place, query, keys, norm, scores, top, mass):
    tokens = query.shape[0]
    mine = place[2]
    own = lax.dot_general(query[...], keys[pl.ds(0, tokens), :], NT, preferred_element_type=F32) * SCALE
    own = jnp.where(causal_of(tokens), own, -jnp.inf)
    scores[0] = own
    top[...] = folded(jnp.maximum, own)
    for at in range(1, len(offsets)):

        @pl.when((mine ^ offsets[at]) < mine)
        def _(at=at):
            value = lax.dot_general(
                query[...], keys[pl.ds(at * tokens, tokens), :], NT, preferred_element_type=F32
            ) * SCALE
            scores[at] = value
            top[...] = jnp.maximum(top[...], folded(jnp.maximum, value))

    peak = jnp.max(top[...], axis=1, keepdims=True)
    mass[...] = folded(jnp.add, jnp.exp2(scores[0] - peak))
    for at in range(1, len(offsets)):

        @pl.when((mine ^ offsets[at]) < mine)
        def _(at=at):
            mass[...] += folded(jnp.add, jnp.exp2(scores[at] - peak))

    total = jnp.sum(mass[...], axis=1, keepdims=True)
    norm[0] = jnp.broadcast_to(peak + jnp.log2(total), (tokens, 128))


def loss_kernel(
    offsets, first, heads, place, query, kept, came, keys, inputs, norm, factor, log_row, log_col, gain_col, out, sums
):
    tokens = query.shape[0]
    mine = place[2]
    causal = causal_of(tokens)
    for i in range(heads):
        head = first + i
        cols = slice(i * HEAD_DIM, (i + 1) * HEAD_DIM)
        asked = query[:, cols]
        read = (kept[:, cols] + came[:, cols].astype(F32)).astype(BF16)
        lse = norm[i]
        wide = tokens // 128
        lse_wide = jnp.concatenate([lse] * wide, axis=1)

        def pair(at):
            rows = pl.ds(at * tokens, tokens)
            score = lax.dot_general(asked, keys[rows, :], NT, preferred_element_type=F32) * SCALE
            inner = lax.dot_general(read, inputs[rows, :], NT, preferred_element_type=F32)
            return jnp.exp2(score - lse_wide), inner * factor[head : head + 1, at * tokens : (at + 1) * tokens]

        prob, inner = pair(0)
        gap = log_col[:, head : head + 1] - log_row[head : head + 1, :]
        diff = jnp.where(causal, prob - inner * jnp.exp2(gap), 0.0)
        sums[...] = folded(jnp.add, diff * diff)
        gain = gain_col[:, head : head + 1]
        for at in range(1, len(offsets)):

            @pl.when((mine ^ offsets[at]) < mine)
            def _(at=at):
                prob, inner = pair(at)
                diff = prob - inner * gain
                sums[...] += folded(jnp.add, diff * diff)

        out[i] = jnp.sum(sums[...].T, axis=0, keepdims=True)


def gather_half(value, half):
    return [value] + [xor_permute(value, "seq", d) for d in range(1, half)]


def activations(hidden, half):
    tokens = hidden.shape[0]
    seq, heads = lax.axis_size("seq"), lax.axis_size("head")
    z, x = lax.axis_index("seq"), lax.axis_index("head")
    side = z // half
    if heads == 2:
        cut = tokens // 2
        spots = [(i, j) for i in range(seq) for j in range(2)]
        flat = lambda i, j: i * 2 + j
        both = ("seq", "head")
        level = side == x
        even = [s for s in spots if s[0] // half == s[1]]
        odd = [s for s in spots if s[0] // half != s[1]]
        over = lambda group: [(flat(i, j), flat(i ^ half, j)) for i, j in group]
        low, high = hidden[:cut], hidden[cut:]
        direct = lax.ppermute(low, both, over(odd))
        swapped = xor_permute(high, "head", 1)
        relayed = lax.ppermute(swapped, both, over(even))
        moved = lax.ppermute(low, both, [(flat(i, j), flat(i, 1 - j)) for i, j in even])
        mine = jnp.where(level, hidden, jnp.concatenate([moved, swapped], axis=0))
        first = jnp.where(level, direct, relayed)
        second = xor_permute(first, "head", 1)
        other = jnp.concatenate([jnp.where(level, first, second), jnp.where(level, second, first)], axis=0)
        return mine, other
    full = lax.all_gather(hidden, "head", axis=1, tiled=True)
    width = full.shape[1] // 2
    share = tokens // heads
    mine = lax.dynamic_slice_in_dim(full, side * width, width, 1)
    sent = lax.dynamic_slice(full, (x * share, (1 - side) * width), (share, width))
    came = xor_permute(sent, "seq", half)
    return mine, lax.all_gather(came, "head", axis=0, tiled=True)


def local(hidden_in, teacher_query, teacher_key, proj_c, proj_b, proj_step, decay_rate):
    _, tokens, _ = hidden_in.shape
    rows, width = proj_c.shape
    head_count = proj_step.shape[1]
    seq = lax.axis_size("seq")
    half = seq // 2
    copies_y, copies_c = lax.axis_size("groups"), lax.axis_size("batch")
    copies = copies_y * copies_c
    z, x = lax.axis_index("seq"), lax.axis_index("head")
    quarter = lax.axis_index("groups") * copies_c + lax.axis_index("batch")
    place = jnp.stack([z % half, quarter, z]).astype(jnp.int32)
    per_model_group = HEADS // KV_HEADS
    group_count = max(1, head_count // per_model_group)
    per_group = head_count // group_count
    group_first = x * head_count // per_model_group
    width_b = group_count * HEAD_DIM
    local_b = lax.dynamic_slice_in_dim(proj_b, group_first * HEAD_DIM, width_b, 1)
    local_key = lax.dynamic_slice_in_dim(teacher_key[0], group_first * HEAD_DIM, width_b, 1)
    offsets = [0, half]
    for d in range(1, half):
        offsets += [d, d ^ half]
    padded = max(16, head_count)

    act_own, act_other = activations(hidden_in[0], half)

    key_pair = jnp.concatenate([local_key, xor_permute(local_key, "seq", half)], axis=0)
    keys = jnp.concatenate(gather_half(key_pair, half), axis=0)

    chunk = max(HEAD_DIM, width // 4)
    count = width // chunk
    part = rows // copies

    def spread(piece):
        got = [piece]
        d = 1
        while d < copies_y:
            got += [xor_permute(g, "groups", d) for g in got]
            d *= 2
        d = 1
        while d < copies_c:
            got += [xor_permute(g, "batch", d) for g in got]
            d *= 2
        return got

    turns = [0]
    d = 1
    while d < copies_y:
        turns += [t ^ (d * copies_c) for t in turns]
        d *= 2
    d = 1
    while d < copies_c:
        turns += [t ^ d for t in turns]
        d *= 2
    model = [(d, t) for d in range(1, half) for t in turns]

    def weights(j):
        piece = lax.dynamic_slice(proj_c, (quarter * part, j * chunk), (part, chunk))
        if j == 0:
            extra = lax.dynamic_slice(local_b, (quarter * part, 0), (part, width_b))
            piece = jnp.concatenate([piece, extra], axis=1)
        return [g for d in range(1, half) for g in spread(xor_permute(piece, "seq", d))]

    pieces = [weights(j) for j in range(count)]
    step_t = jnp.pad(proj_step.T, ((0, padded - head_count), (0, 0)))
    step_pieces = gather_half(step_t, half)

    def partial(act, j, dtype):
        specs = [smem(), whole(act.shape), columns(rows, chunk, j)] + [columns(part, chunk, 0)] * len(model)
        return call(
            functools.partial(partial_kernel, model),
            (place, act, proj_c, *pieces[j]),
            specs,
            [jax.ShapeDtypeStruct((tokens, chunk), dtype)],
            "partial",
        )[0]

    extra_out = [
        jax.ShapeDtypeStruct((2 * tokens, width_b), F32),
        jax.ShapeDtypeStruct((2 * tokens, width_b), BF16),
        jax.ShapeDtypeStruct((padded, 2 * tokens), F32),
    ]
    extra_cols = [g[:, chunk:] for g in pieces[0]]
    full, rounded, raw = call(
        functools.partial(extra_kernel, model, list(range(half))),
        (place, act_own, act_other, local_b, *extra_cols, *step_pieces),
        [smem(), whole(act_own.shape), whole(act_other.shape), whole(local_b.shape)]
        + [whole((part, width_b))] * len(model)
        + [whole(step_t.shape)] * half,
        extra_out,
        "extra",
    )
    came = xor_permute(rounded, "seq", half).astype(F32)
    came_raw = xor_permute(raw, "seq", half)
    inputs_pair = (full + jnp.concatenate([came[tokens:], came[:tokens]], axis=0)).astype(BF16)
    raw_pair = raw + jnp.concatenate([came_raw[:, tokens:], came_raw[:, :tokens]], axis=1)
    inputs = jnp.concatenate(gather_half(inputs_pair, half), axis=0)
    raw_all = jnp.stack([r[:, i * tokens : (i + 1) * tokens] for r in gather_half(raw_pair, half) for i in range(2)])

    sent = [partial(act_other, j, BF16) for j in range(count)]
    arrived = [xor_permute(s, "seq", half) for s in sent]
    kept = [partial(act_own, j, F32) for j in range(count)]

    span = seq * tokens
    rate = jnp.pad(decay_rate, (0, padded - head_count))[:, None]
    factor, log_row, log_col, gain_col = call(
        functools.partial(decay_kernel, offsets),
        (place, raw_all, rate),
        [smem(), whole(raw_all.shape), whole(rate.shape)],
        [
            jax.ShapeDtypeStruct((padded, span), F32),
            jax.ShapeDtypeStruct((padded, tokens), F32),
            jax.ShapeDtypeStruct((tokens, 128), F32),
            jax.ShapeDtypeStruct((tokens, 128), F32),
        ],
        "decay",
    )
    query = teacher_query[0]
    norm = pl.pallas_call(
        functools.partial(teacher_kernel, offsets),
        grid=(head_count,),
        in_specs=[
            smem(),
            pl.BlockSpec((tokens, HEAD_DIM), lambda h: (0, h)),
            pl.BlockSpec((span, HEAD_DIM), lambda h: (0, h // per_group)),
        ],
        out_specs=pl.BlockSpec((1, tokens, 128), lambda h: (h, 0, 0)),
        out_shape=jax.ShapeDtypeStruct((head_count, tokens, 128), F32),
        scratch_shapes=[
            pltpu.VMEM((seq, tokens, tokens), F32),
            pltpu.VMEM((tokens, 128), F32),
            pltpu.VMEM((tokens, 128), F32),
        ],
        compiler_params=pltpu.CompilerParams(vmem_limit_bytes=VMEM_LIMIT),
        name="teacher",
    )(place, query, keys)

    heads = chunk // HEAD_DIM
    losses = []
    for j in range(count):
        group = j * heads // per_group
        losses.append(
            call(
                functools.partial(loss_kernel, offsets, j * heads, heads),
                (place, query, kept[j], arrived[j], keys, inputs, norm, factor, log_row, log_col, gain_col),
                [
                    smem(),
                    columns(tokens, chunk, j),
                    whole((tokens, chunk)),
                    whole((tokens, chunk)),
                    columns(span, HEAD_DIM, group),
                    columns(span, HEAD_DIM, group),
                    pl.BlockSpec((heads, tokens, 128), lambda *_, j=j: (j, 0, 0)),
                    whole(factor.shape),
                    whole(log_row.shape),
                    whole(log_col.shape),
                    whole(gain_col.shape),
                ],
                [jax.ShapeDtypeStruct((heads, 1, tokens), F32)],
                "loss",
                [pltpu.VMEM((tokens, 128), F32)],
            )[0]
        )
    return jnp.concatenate(losses, axis=0).reshape(1, head_count, tokens)


def solution(mesh):
    in_specs = (
        P(("groups", "batch"), "seq", "head"),
        P(("groups", "batch"), "seq", "head"),
        P(("groups", "batch"), "seq", None),
        P("seq", "head"),
        P("seq", None),
        P("seq", "head"),
        P("head"),
    )
    out_specs = P(("groups", "batch"), "head", "seq")
    return jax.shard_map(local, mesh=mesh, in_specs=in_specs, out_specs=out_specs, check_vma=False)
```

```python
import functools
import math

import jax
import jax.numpy as jnp
from jax import lax
from jax.experimental import pallas as pl
from jax.experimental.pallas import tpu as pltpu
from jax.sharding import PartitionSpec as P

HEADS = 32
KV_HEADS = 4
HEAD_DIM = 128
LOG2E = math.log2(math.e)
BF16 = jnp.bfloat16
F32 = jnp.float32
VMEM_LIMIT = 48 * 1024 * 1024

NT = (((1,), (1,)), ((), ()))


def xor_permute(value, axis, offset):
    size = lax.axis_size(axis)
    return lax.ppermute(value, axis, [(i, i ^ offset) for i in range(size)])


def whole(shape):
    return pl.BlockSpec(shape, lambda *_: (0,) * len(shape))


def columns(rows, width, index):
    return pl.BlockSpec((rows, width), lambda *_: (0, index))


def smem():
    return pl.BlockSpec(memory_space=pltpu.SMEM)


def call(kernel, args, in_specs, out_shapes, name, scratch=()):
    return pl.pallas_call(
        kernel,
        grid=(1,),
        in_specs=in_specs,
        out_specs=tuple(whole(s.shape) for s in out_shapes),
        out_shape=tuple(out_shapes),
        scratch_shapes=list(scratch),
        compiler_params=pltpu.CompilerParams(vmem_limit_bytes=VMEM_LIMIT),
        name=name,
    )(*args)


def product(place, act, own, pieces, model):
    block, quarter = place[0], place[1]
    rows = own.shape[0]
    total = jnp.dot(
        act[:, pl.ds(pl.multiple_of(block * rows, rows), rows)], own[...], preferred_element_type=F32
    )
    for piece, (step, turn) in zip(pieces, model):
        part = piece.shape[0]
        start = (block ^ step) * rows + (quarter ^ turn) * part
        total += jnp.dot(
            act[:, pl.ds(pl.multiple_of(start, part), part)], piece[...], preferred_element_type=F32
        )
    return total


def partial_kernel(model, number, place, *rest):
    acts, own, pieces, outs = rest[:number], rest[number], rest[number + 1 : -number], rest[-number:]
    for act, out in zip(acts, outs):
        out[...] = product(place, act, own, pieces, model).astype(out.dtype)


def extra_kernel(model, step_model, place, act_own, act_low, act_high, own, *rest):
    n = len(model)
    pieces = rest[:n]
    step_pieces = rest[n : n + len(step_model)]
    full, rounded, raw = rest[-3:]
    first = 0
    for act in (act_own, act_low, act_high):
        here = slice(first, first + act.shape[0])
        first += act.shape[0]
        value = product(place, act, own, pieces, model)
        full[here, :] = value
        rounded[here, :] = value.astype(BF16)
        total = None
        for piece, step in zip(step_pieces, step_model):
            rows = piece.shape[1]
            start = pl.multiple_of((place[0] ^ step) * rows, rows)
            part = lax.dot_general(piece[...], act[:, pl.ds(start, rows)], NT, preferred_element_type=F32)
            total = part if total is None else total + part
        raw[:, here] = total


def decay_kernel(offsets, place, raw, rate, factor, log_row, log_col, gain_col):
    mine = place[2]
    heads, tokens = raw.shape[1], raw.shape[2]
    lane = lax.broadcasted_iota(jnp.int32, (heads, tokens), 1)
    steps, logs, totals = [], [], []
    for at in range(len(offsets)):
        value = raw[at]
        step = jnp.maximum(value, 0.0) + jnp.log1p(jnp.exp(-jnp.abs(value)))
        log = step * (-LOG2E * rate[...])
        shift = 1
        while shift < tokens:
            log = log + jnp.where(lane >= shift, pltpu.roll(log, shift, 1), 0.0)
            shift *= 2
        steps.append(step)
        logs.append(log)
        totals.append(log[:, tokens - 1 :])
    for at, offset in enumerate(offsets):
        here = slice(at * tokens, (at + 1) * tokens)
        if at == 0:
            factor[:, here] = steps[0]
            continue
        between = jnp.zeros_like(totals[0])
        first = mine ^ offset
        for other, distance in enumerate(offsets):
            block = mine ^ distance
            inside = jnp.logical_and(block > first, block < mine)
            between += jnp.where(inside, totals[other], 0.0)
        factor[:, here] = steps[at] * jnp.exp2(totals[at] - logs[at] + between)
    log_row[...] = logs[0]
    wide = jnp.concatenate([logs[0], jnp.zeros((128 - heads, tokens), F32)], axis=0)
    turned = wide.T
    log_col[...] = turned
    gain_col[...] = jnp.exp2(turned)


def causal_of(tokens):
    row = lax.broadcasted_iota(jnp.int32, (tokens, tokens), 0)
    col = lax.broadcasted_iota(jnp.int32, (tokens, tokens), 1)
    return col <= row


def folded(combine, value):
    parts = [value[:, i : i + 128] for i in range(0, value.shape[1], 128)]
    return functools.reduce(combine, parts)


SCALE = LOG2E * HEAD_DIM ** -0.5


def teacher_kernel(offsets, place, query, keys, norm, scores, top, mass):
    tokens = query.shape[0]
    mine = place[2]
    own = lax.dot_general(query[...], keys[pl.ds(0, tokens), :], NT, preferred_element_type=F32) * SCALE
    own = jnp.where(causal_of(tokens), own, -jnp.inf)
    scores[0] = own
    top[...] = folded(jnp.maximum, own)
    for at in range(1, len(offsets)):

        @pl.when((mine ^ offsets[at]) < mine)
        def _(at=at):
            value = lax.dot_general(
                query[...], keys[pl.ds(at * tokens, tokens), :], NT, preferred_element_type=F32
            ) * SCALE
            scores[at] = value
            top[...] = jnp.maximum(top[...], folded(jnp.maximum, value))

    peak = jnp.max(top[...], axis=1, keepdims=True)
    mass[...] = folded(jnp.add, jnp.exp2(scores[0] - peak))
    for at in range(1, len(offsets)):

        @pl.when((mine ^ offsets[at]) < mine)
        def _(at=at):
            mass[...] += folded(jnp.add, jnp.exp2(scores[at] - peak))

    total = jnp.sum(mass[...], axis=1, keepdims=True)
    norm[0] = jnp.broadcast_to(peak + jnp.log2(total), (tokens, 128))


def loss_kernel(
    offsets, first, heads, place, query, kept, came_low, came_high, keys, inputs, norm, factor, log_row, log_col, gain_col, out, sums
):
    tokens = query.shape[0]
    mine = place[2]
    causal = causal_of(tokens)
    for i in range(heads):
        head = first + i
        cols = slice(i * HEAD_DIM, (i + 1) * HEAD_DIM)
        asked = query[:, cols]
        came = jnp.concatenate([came_low[:, cols], came_high[:, cols]], axis=0)
        read = (kept[:, cols] + came.astype(F32)).astype(BF16)
        lse = norm[i]
        wide = tokens // 128
        lse_wide = jnp.concatenate([lse] * wide, axis=1)

        def pair(at):
            rows = pl.ds(at * tokens, tokens)
            score = lax.dot_general(asked, keys[rows, :], NT, preferred_element_type=F32) * SCALE
            inner = lax.dot_general(read, inputs[rows, :], NT, preferred_element_type=F32)
            return jnp.exp2(score - lse_wide), inner * factor[head : head + 1, at * tokens : (at + 1) * tokens]

        prob, inner = pair(0)
        gap = log_col[:, head : head + 1] - log_row[head : head + 1, :]
        diff = jnp.where(causal, prob - inner * jnp.exp2(gap), 0.0)
        sums[...] = folded(jnp.add, diff * diff)
        gain = gain_col[:, head : head + 1]
        for at in range(1, len(offsets)):

            @pl.when((mine ^ offsets[at]) < mine)
            def _(at=at):
                prob, inner = pair(at)
                diff = prob - inner * gain
                sums[...] += folded(jnp.add, diff * diff)

        out[i] = jnp.sum(sums[...].T, axis=0, keepdims=True)


class Order:
    def __init__(self):
        self.last = ()

    def gate(self, value):
        if not self.last:
            return value
        value, self.last = lax.optimization_barrier((value, self.last))
        return value

    def wait(self, value):
        value, _ = lax.optimization_barrier((value, self.last))
        self.last = tuple(jax.tree.leaves(value))
        return value


def xor_sums(offset_size, scale):
    got = [0]
    d = 1
    while d < offset_size:
        got += [g ^ (d * scale) for g in got]
        d *= 2
    return got


def spread(pieces, axis):
    got = list(pieces)
    d = 1
    while d < lax.axis_size(axis):
        got += [xor_permute(g, axis, d) for g in got]
        d *= 2
    return got


def local(hidden_in, teacher_query, teacher_key, proj_c, proj_b, proj_step, decay_rate):
    _, tokens, _ = hidden_in.shape
    hidden = hidden_in[0]
    rows, width = proj_c.shape
    head_count = proj_step.shape[1]
    seq, sides = lax.axis_size("seq"), lax.axis_size("head")
    half = seq // 2
    copies_y, copies_c = lax.axis_size("groups"), lax.axis_size("batch")
    copies = copies_y * copies_c
    z, x = lax.axis_index("seq"), lax.axis_index("head")
    side = z // half
    quarter = lax.axis_index("groups") * copies_c + lax.axis_index("batch")
    place = jnp.stack([z % half, quarter, z]).astype(jnp.int32)
    per_model_group = HEADS // KV_HEADS
    group_count = max(1, head_count // per_model_group)
    per_group = head_count // group_count
    group_first = x * head_count // per_model_group
    width_b = group_count * HEAD_DIM
    offsets = [0, half]
    for d in range(1, half):
        offsets += [d, d ^ half]
    padded = max(16, head_count)
    span = seq * tokens
    chunk = max(HEAD_DIM, width // 4)
    count = width // chunk
    heads = chunk // HEAD_DIM
    part = rows // copies
    turns = xor_sums(copies_y, copies_c)
    turns = [t ^ c for c in xor_sums(copies_c, 1) for t in turns]
    model = [(d, t) for d in range(1, half) for t in turns]
    query = teacher_query[0]
    order = Order()

    def over_half(value):
        return [xor_permute(value, "seq", d) for d in range(1, half)]

    def start_weights(first, last):
        piece = lax.dynamic_slice(proj_c, (quarter * part, first * chunk), (part, (last - first) * chunk))
        if first == 0:
            extra = lax.dynamic_slice(proj_b, (quarter * part, group_first * HEAD_DIM), (part, width_b))
            piece = jnp.concatenate([piece, extra], axis=1)
        return over_half(piece)

    def partial(acts, j):
        first, _, pieces = next(w for w in weights if w[0] <= j < w[1])
        return order.wait(
            call(
                functools.partial(partial_kernel, model, len(acts)),
                (order.gate(place), *[a for a, _ in acts], proj_c, *pieces),
                [smem()]
                + [whole(a.shape) for a, _ in acts]
                + [columns(rows, chunk, j)]
                + [columns(part, chunk, j - first)] * len(model),
                [jax.ShapeDtypeStruct((a.shape[0], chunk), dtype) for a, dtype in acts],
                "partial",
            )
        )

    def send(value):
        return xor_permute(value, "seq", half)

    def teacher(first, number):
        return pl.pallas_call(
            functools.partial(teacher_kernel, offsets),
            grid=(number,),
            in_specs=[
                smem(),
                pl.BlockSpec((tokens, HEAD_DIM), lambda h: (0, first + h)),
                pl.BlockSpec((span, HEAD_DIM), lambda h: (0, (first + h) // per_group)),
            ],
            out_specs=pl.BlockSpec((1, tokens, 128), lambda h: (h, 0, 0)),
            out_shape=jax.ShapeDtypeStruct((number, tokens, 128), F32),
            scratch_shapes=[
                pltpu.VMEM((seq, tokens, tokens), F32),
                pltpu.VMEM((tokens, 128), F32),
                pltpu.VMEM((tokens, 128), F32),
            ],
            compiler_params=pltpu.CompilerParams(vmem_limit_bytes=VMEM_LIMIT),
            name="teacher",
        )(order.gate(place), query, keys)

    spans = [(0, 1), (1, 2), (2, 4)]
    weights = []
    local_key = lax.dynamic_slice_in_dim(teacher_key[0], group_first * HEAD_DIM, width_b, 1)
    local_b = lax.dynamic_slice_in_dim(proj_b, group_first * HEAD_DIM, width_b, 1)
    step_t = jnp.pad(proj_step.T, ((0, padded - head_count), (0, 0)))

    if sides == 2:
        cut = tokens // 4
        spots = [(i, j) for i in range(seq) for j in range(2)]
        flat = lambda i, j: i * 2 + j
        both = ("seq", "head")
        level = side == x
        even = [s for s in spots if s[0] // half == s[1]]
        odd = [s for s in spots if s[0] // half != s[1]]
        over = lambda value, group: lax.ppermute(value, both, [(flat(i, j), flat(i ^ half, j)) for i, j in group])
        row = [hidden[i * cut : (i + 1) * cut] for i in range(4)]
        across = lambda value: lax.ppermute(value, both, [(flat(i, j), flat(i, 1 - j)) for i, j in even])
        direct = [over(row[0], odd), over(row[2], odd)]
        swapped = [xor_permute(row[1], "head", 1), xor_permute(row[3], "head", 1)]
        key_half = xor_permute(local_key, "seq", half)
        w0 = start_weights(0, 1)
        w1 = start_weights(1, 2)
        w2 = start_weights(2, 4)
        step_rest = over_half(step_t)
        swapped[0] = order.wait(swapped[0])
        relayed = [over(swapped[0], even), None]
        swapped[1] = order.wait(swapped[1])
        relayed[1] = over(swapped[1], even)
        moved = [across(order.gate(row[0])), None]
        w0 = spread(order.wait(w0), "groups")

        def swap(i):
            got = order.wait((direct[i], relayed[i]))
            first = jnp.where(level, got[0], got[1])
            return first, xor_permute(first, "head", 1)

        def join(first, second):
            second = order.wait(second)
            return jnp.concatenate([jnp.where(level, first, second), jnp.where(level, second, first)], axis=0)

        first0, second0 = swap(0)
        moved[0] = order.wait(moved[0])
        moved[1] = across(order.gate(row[2]))
        w0 = spread(order.wait(w0), "batch")
        w1 = spread(order.wait(w1), "groups")
        others = [join(first0, second0)]
        weights.append((0, 1, order.wait(w0)))
        arrived = {(0, 0): send(partial([(others[0], BF16)], 0)[0])}
        first1, second1 = swap(1)
        moved[1] = order.wait(moved[1])
        w1 = spread(order.wait(w1), "batch")
        key_half = order.wait(key_half)
        key_pair = jnp.concatenate([local_key, key_half], axis=0)
        key_rest = over_half(key_pair)
        w2 = spread(order.wait(w2), "groups")
        mine = jnp.where(
            level, hidden, jnp.concatenate([moved[0], swapped[0], moved[1], swapped[1]], axis=0)
        )
        weights.append((1, 2, order.wait(w1)))
        arrived[0, 1] = send(partial([(others[0], BF16)], 1)[0])
        step_rest = order.wait(step_rest)
        others.append(join(first1, second1))
        norms = []
    else:
        full = lax.all_gather(hidden, "head", axis=1, tiled=True)
        span_half = full.shape[1] // 2
        share = tokens // sides
        mine = lax.dynamic_slice_in_dim(full, side * span_half, span_half, 1)
        leaving = lax.dynamic_slice(full, (x * share, (1 - side) * span_half), (share, span_half))
        came = lax.all_gather(xor_permute(leaving, "seq", half), "head", axis=0, tiled=True)
        others = [came[: tokens // 2], came[tokens // 2 :]]
        key_pair = jnp.concatenate([local_key, xor_permute(local_key, "seq", half)], axis=0)
        step_rest = over_half(step_t)
        weights.append((0, 1, spread(spread(start_weights(0, 1), "groups"), "batch")))
        weights.append((1, 2, spread(spread(start_weights(1, 2), "groups"), "batch")))
        w2 = spread(start_weights(2, 4), "groups")
        norms = []
        key_rest = over_half(key_pair)
        arrived = {(0, j): send(partial([(others[0], BF16)], j)[0]) for j in range(2)}

    extra_out = [
        jax.ShapeDtypeStruct((2 * tokens, width_b), F32),
        jax.ShapeDtypeStruct((2 * tokens, width_b), BF16),
        jax.ShapeDtypeStruct((padded, 2 * tokens), F32),
    ]
    extra_cols = [g[:, chunk:] for g in weights[0][2]]
    acts = (mine, *others)
    full, rounded, raw = order.wait(
        call(
            functools.partial(extra_kernel, model, list(range(half))),
            (order.gate(place), *acts, local_b, *extra_cols, step_t, *step_rest),
            [smem()]
            + [whole(a.shape) for a in acts]
            + [whole(local_b.shape)]
            + [whole((part, width_b))] * len(model)
            + [whole(step_t.shape)] * half,
            extra_out,
            "extra",
        )
    )
    came = send(rounded)
    came_raw = send(raw)
    kept = []
    for j in range(2):
        leaving, stays = partial([(others[1], BF16), (mine, F32)], j)
        arrived[1, j] = send(leaving)
        kept.append(stays)
    w2 = spread(order.wait(w2), "batch")
    key_rest = order.wait(key_rest)
    keys = jnp.concatenate([key_pair] + key_rest, axis=0)
    norms.append(order.wait(teacher(0, heads)))
    came, came_raw = order.wait((came, came_raw))
    came = came.astype(F32)
    inputs_pair = (full + jnp.concatenate([came[tokens:], came[:tokens]], axis=0)).astype(BF16)
    raw_pair = raw + jnp.concatenate([came_raw[:, tokens:], came_raw[:, :tokens]], axis=1)
    inputs_rest = over_half(inputs_pair)
    raw_rest = over_half(raw_pair)
    norms.append(order.wait(teacher(heads, heads)))
    weights.append((2, 4, order.wait(w2)))
    for j in range(2, count):
        if j == count - 1:
            inputs_rest, raw_rest = order.wait((inputs_rest, raw_rest))
        low, high, stays = partial([(others[0], BF16), (others[1], BF16), (mine, F32)], j)
        arrived[0, j], arrived[1, j] = send(low), send(high)
        kept.append(stays)
        norms.append(order.wait(teacher(j * heads, heads)))
    inputs = jnp.concatenate([inputs_pair] + inputs_rest, axis=0)
    raw_all = jnp.stack([r[:, i * tokens : (i + 1) * tokens] for r in [raw_pair] + raw_rest for i in range(2)])
    rate = jnp.pad(decay_rate, (0, padded - head_count))[:, None]
    factor, log_row, log_col, gain_col = call(
        functools.partial(decay_kernel, offsets),
        (order.gate(place), raw_all, rate),
        [smem(), whole(raw_all.shape), whole(rate.shape)],
        [
            jax.ShapeDtypeStruct((padded, span), F32),
            jax.ShapeDtypeStruct((padded, tokens), F32),
            jax.ShapeDtypeStruct((tokens, 128), F32),
            jax.ShapeDtypeStruct((tokens, 128), F32),
        ],
        "decay",
    )
    factor = order.wait(factor)

    losses = []
    for j in range(count):
        group = j * heads // per_group
        came = order.wait((arrived[0, j], arrived[1, j]))
        losses.append(
            order.wait(
                call(
                    functools.partial(loss_kernel, offsets, j * heads, heads),
                    (place, query, kept[j], *came, keys, inputs, norms[j], factor, log_row, log_col, gain_col),
                    [
                        smem(),
                        columns(tokens, chunk, j),
                        whole((tokens, chunk)),
                        whole((tokens // 2, chunk)),
                        whole((tokens // 2, chunk)),
                        columns(span, HEAD_DIM, group),
                        columns(span, HEAD_DIM, group),
                        whole(norms[j].shape),
                        whole(factor.shape),
                        whole(log_row.shape),
                        whole(log_col.shape),
                        whole(gain_col.shape),
                    ],
                    [jax.ShapeDtypeStruct((heads, 1, tokens), F32)],
                    "loss",
                    [pltpu.VMEM((tokens, 128), F32)],
                )[0]
            )
        )
    return jnp.concatenate(losses, axis=0).reshape(1, head_count, tokens)


def solution(mesh):
    in_specs = (
        P(("groups", "batch"), "seq", "head"),
        P(("groups", "batch"), "seq", "head"),
        P(("groups", "batch"), "seq", None),
        P("seq", "head"),
        P("seq", None),
        P("seq", "head"),
        P("head"),
    )
    out_specs = P(("groups", "batch"), "head", "seq")
    return jax.shard_map(local, mesh=mesh, in_specs=in_specs, out_specs=out_specs, check_vma=False)
```

```python
import functools
import math

import jax
import jax.numpy as jnp
from jax import lax
from jax.experimental import pallas as pl
from jax.experimental.pallas import tpu as pltpu
from jax.sharding import PartitionSpec as P

HEADS = 32
KV_HEADS = 4
HEAD_DIM = 128
LOG2E = math.log2(math.e)
BF16 = jnp.bfloat16
F32 = jnp.float32
VMEM_LIMIT = 48 * 1024 * 1024

NT = (((1,), (1,)), ((), ()))


def xor_permute(value, axis, offset):
    size = lax.axis_size(axis)
    return lax.ppermute(value, axis, [(i, i ^ offset) for i in range(size)])


def whole(shape):
    return pl.BlockSpec(shape, lambda *_: (0,) * len(shape))


def columns(rows, width, index):
    return pl.BlockSpec((rows, width), lambda *_: (0, index))


def smem():
    return pl.BlockSpec(memory_space=pltpu.SMEM)


def call(kernel, args, in_specs, out_shapes, name, scratch=()):
    return pl.pallas_call(
        kernel,
        grid=(1,),
        in_specs=in_specs,
        out_specs=tuple(whole(s.shape) for s in out_shapes),
        out_shape=tuple(out_shapes),
        scratch_shapes=list(scratch),
        compiler_params=pltpu.CompilerParams(vmem_limit_bytes=VMEM_LIMIT),
        name=name,
    )(*args)


def product(place, act, own, pieces, model):
    block, quarter = place[0], place[1]
    rows = own.shape[0]
    total = jnp.dot(
        act[:, pl.ds(pl.multiple_of(block * rows, rows), rows)], own[...], preferred_element_type=F32
    )
    for piece, (step, turn) in zip(pieces, model):
        part = piece.shape[0]
        start = (block ^ step) * rows + (quarter ^ turn) * part
        total += jnp.dot(
            act[:, pl.ds(pl.multiple_of(start, part), part)], piece[...], preferred_element_type=F32
        )
    return total


def partial_kernel(model, groups, place, *rest):
    number = sum(groups)
    acts, own, pieces, outs = rest[:number], rest[number], rest[number + 1 : -len(groups)], rest[-len(groups) :]
    acts = list(acts)
    for size, out in zip(groups, outs):
        row = 0
        for act in acts[:size]:
            out[row : row + act.shape[0], :] = product(place, act, own, pieces, model).astype(out.dtype)
            row += act.shape[0]
        del acts[:size]


def extra_kernel(model, step_model, place, act_own, act_low, act_high, own, *rest):
    n = len(model)
    pieces = rest[:n]
    step_pieces = rest[n : n + len(step_model)]
    full, rounded, raw = rest[-3:]
    first = 0
    for act in (act_own, act_low, act_high):
        here = slice(first, first + act.shape[0])
        first += act.shape[0]
        value = product(place, act, own, pieces, model)
        full[here, :] = value
        rounded[here, :] = value.astype(BF16)
        total = None
        for piece, step in zip(step_pieces, step_model):
            rows = piece.shape[1]
            start = pl.multiple_of((place[0] ^ step) * rows, rows)
            part = lax.dot_general(piece[...], act[:, pl.ds(start, rows)], NT, preferred_element_type=F32)
            total = part if total is None else total + part
        raw[:, here] = total


def decay_kernel(offsets, place, raw, rate, factor, log_row, log_col, gain_col):
    mine = place[2]
    heads, tokens = raw.shape[1], raw.shape[2]
    lane = lax.broadcasted_iota(jnp.int32, (heads, tokens), 1)
    steps, logs, totals = [], [], []
    for at in range(len(offsets)):
        value = raw[at]
        step = jnp.maximum(value, 0.0) + jnp.log1p(jnp.exp(-jnp.abs(value)))
        log = step * (-LOG2E * rate[...])
        shift = 1
        while shift < tokens:
            log = log + jnp.where(lane >= shift, pltpu.roll(log, shift, 1), 0.0)
            shift *= 2
        steps.append(step)
        logs.append(log)
        totals.append(log[:, tokens - 1 :])
    for at, offset in enumerate(offsets):
        here = slice(at * tokens, (at + 1) * tokens)
        if at == 0:
            factor[:, here] = steps[0]
            continue
        between = jnp.zeros_like(totals[0])
        first = mine ^ offset
        for other, distance in enumerate(offsets):
            block = mine ^ distance
            inside = jnp.logical_and(block > first, block < mine)
            between += jnp.where(inside, totals[other], 0.0)
        factor[:, here] = steps[at] * jnp.exp2(totals[at] - logs[at] + between)
    log_row[...] = logs[0]
    wide = jnp.concatenate([logs[0], jnp.zeros((128 - heads, tokens), F32)], axis=0)
    turned = wide.T
    log_col[...] = turned
    gain_col[...] = jnp.exp2(turned)


def causal_of(tokens):
    row = lax.broadcasted_iota(jnp.int32, (tokens, tokens), 0)
    col = lax.broadcasted_iota(jnp.int32, (tokens, tokens), 1)
    return col <= row


def folded(combine, value):
    parts = [value[:, i : i + 128] for i in range(0, value.shape[1], 128)]
    return functools.reduce(combine, parts)


SCALE = LOG2E * HEAD_DIM ** -0.5


def for_place(mine, offsets, body):
    for position in range(len(offsets)):
        earlier = [at for at in range(1, len(offsets)) if (position ^ offsets[at]) < position]
        pl.when(mine == position)(functools.partial(body, earlier))


def teacher_kernel(offsets, place, query, keys, norm):
    tokens = query.shape[0]

    def body(earlier):
        asked = query[...]
        scores = []
        for at in [0] + earlier:
            key = keys[pl.ds(at * tokens, tokens), :]
            scores.append(lax.dot_general(asked, key, NT, preferred_element_type=F32) * SCALE)
        scores[0] = jnp.where(causal_of(tokens), scores[0], -jnp.inf)
        top = functools.reduce(jnp.maximum, [folded(jnp.maximum, s) for s in scores])
        peak = jnp.max(top, axis=1, keepdims=True)
        mass = functools.reduce(jnp.add, [folded(jnp.add, jnp.exp2(s - peak)) for s in scores])
        total = jnp.sum(mass, axis=1, keepdims=True)
        norm[0] = jnp.broadcast_to(peak + jnp.log2(total), (tokens, 128))

    for_place(place[2], offsets, body)


def loss_kernel(
    offsets, first, heads, place, query, kept, keys, inputs, norm, factor, log_row, log_col, gain_col, *rest
):
    arrived, out = rest[:-1], rest[-1]
    tokens = query.shape[0]

    lane = lax.broadcasted_iota(jnp.int32, (tokens, 128), 1)

    def body(earlier):
        def one_head(i, carry):
            head = first + i
            cols = pl.ds(pl.multiple_of(i * HEAD_DIM, HEAD_DIM), HEAD_DIM)

            def column(ref):
                return jnp.sum(jnp.where(lane == head, ref[...], 0.0), axis=1, keepdims=True)

            asked = query[:, cols]
            came = jnp.concatenate([a[:, cols] for a in arrived], axis=0)
            read = (kept[:, cols] + came.astype(F32)).astype(BF16)
            lse = jnp.concatenate([norm[i]] * (tokens // 128), axis=1)
            gain = column(gain_col)
            sums = None
            for at in [0] + earlier:
                rows = pl.ds(at * tokens, tokens)
                score = lax.dot_general(asked, keys[rows, :], NT, preferred_element_type=F32) * SCALE
                inner = lax.dot_general(read, inputs[rows, :], NT, preferred_element_type=F32)
                inner = inner * factor[pl.ds(head, 1), at * tokens : (at + 1) * tokens]
                prob = jnp.exp2(score - lse)
                if at == 0:
                    gap = column(log_col) - log_row[pl.ds(head, 1), :]
                    diff = jnp.where(causal_of(tokens), prob - inner * jnp.exp2(gap), 0.0)
                else:
                    diff = prob - inner * gain
                square = folded(jnp.add, diff * diff)
                sums = square if sums is None else sums + square
            out[i] = jnp.sum(sums.T, axis=0, keepdims=True)
            return carry

        lax.fori_loop(0, heads, one_head, 0)

    for_place(place[2], offsets, body)


class Order:
    def __init__(self):
        self.last = ()

    def gate(self, value):
        if not self.last:
            return value
        value, self.last = lax.optimization_barrier((value, self.last))
        return value

    def wait(self, value):
        value, _ = lax.optimization_barrier((value, self.last))
        self.last = tuple(jax.tree.leaves(value))
        return value


def xor_sums(offset_size, scale):
    got = [0]
    d = 1
    while d < offset_size:
        got += [g ^ (d * scale) for g in got]
        d *= 2
    return got


def spread(pieces, axis):
    got = list(pieces)
    d = 1
    while d < lax.axis_size(axis):
        got += [xor_permute(g, axis, d) for g in got]
        d *= 2
    return got


def local(hidden_in, teacher_query, teacher_key, proj_c, proj_b, proj_step, decay_rate):
    _, tokens, _ = hidden_in.shape
    hidden = hidden_in[0]
    rows, width = proj_c.shape
    head_count = proj_step.shape[1]
    seq, sides = lax.axis_size("seq"), lax.axis_size("head")
    half = seq // 2
    copies_y, copies_c = lax.axis_size("groups"), lax.axis_size("batch")
    copies = copies_y * copies_c
    z, x = lax.axis_index("seq"), lax.axis_index("head")
    side = z // half
    quarter = lax.axis_index("groups") * copies_c + lax.axis_index("batch")
    place = jnp.stack([z % half, quarter, z]).astype(jnp.int32)
    per_model_group = HEADS // KV_HEADS
    group_count = max(1, head_count // per_model_group)
    per_group = head_count // group_count
    group_first = x * head_count // per_model_group
    width_b = group_count * HEAD_DIM
    offsets = [0, half]
    for d in range(1, half):
        offsets += [d, d ^ half]
    padded = max(16, head_count)
    span = seq * tokens
    chunk = max(HEAD_DIM, width // 4)
    count = width // chunk
    heads = chunk // HEAD_DIM
    part = rows // copies
    turns = xor_sums(copies_y, copies_c)
    turns = [t ^ c for c in xor_sums(copies_c, 1) for t in turns]
    model = [(d, t) for d in range(1, half) for t in turns]
    query = teacher_query[0]
    order = Order()

    def over_half(value):
        return [xor_permute(value, "seq", d) for d in range(1, half)]

    def start_weights(first, last):
        piece = lax.dynamic_slice(proj_c, (quarter * part, first * chunk), (part, (last - first) * chunk))
        if first == 0:
            extra = lax.dynamic_slice(proj_b, (quarter * part, group_first * HEAD_DIM), (part, width_b))
            piece = jnp.concatenate([piece, extra], axis=1)
        return over_half(piece)

    def send(value):
        return xor_permute(value, "seq", half)

    def partial(acts, j):
        first, _, pieces = next(w for w in weights if w[0] <= j < w[1])
        flat_acts = [a for blocks, _ in acts for a in blocks]
        return order.wait(
            call(
                functools.partial(partial_kernel, model, [len(blocks) for blocks, _ in acts]),
                (order.gate(place), *flat_acts, proj_c, *pieces),
                [smem()]
                + [whole(a.shape) for a in flat_acts]
                + [columns(rows, chunk, j)]
                + [columns(part, chunk, j - first)] * len(model),
                [jax.ShapeDtypeStruct((sum(a.shape[0] for a in blocks), chunk), dtype) for blocks, dtype in acts],
                "partial",
            )
        )

    def teacher(first, number):
        return pl.pallas_call(
            functools.partial(teacher_kernel, offsets),
            grid=(number,),
            in_specs=[
                smem(),
                pl.BlockSpec((tokens, HEAD_DIM), lambda h: (0, first + h)),
                pl.BlockSpec((span, HEAD_DIM), lambda h: (0, (first + h) // per_group)),
            ],
            out_specs=pl.BlockSpec((1, tokens, 128), lambda h: (h, 0, 0)),
            out_shape=jax.ShapeDtypeStruct((number, tokens, 128), F32),
            compiler_params=pltpu.CompilerParams(vmem_limit_bytes=VMEM_LIMIT),
            name="teacher",
        )(order.gate(place), query, keys)

    spans = [(0, 1), (1, 2), (2, 4)]
    weights = []
    local_key = lax.dynamic_slice_in_dim(teacher_key[0], group_first * HEAD_DIM, width_b, 1)
    local_b = lax.dynamic_slice_in_dim(proj_b, group_first * HEAD_DIM, width_b, 1)
    step_t = jnp.pad(proj_step.T, ((0, padded - head_count), (0, 0)))

    if sides == 2:
        cut = tokens // 4
        spots = [(i, j) for i in range(seq) for j in range(2)]
        flat = lambda i, j: i * 2 + j
        both = ("seq", "head")
        level = side == x
        even = [s for s in spots if s[0] // half == s[1]]
        odd = [s for s in spots if s[0] // half != s[1]]
        over = lambda value, group: lax.ppermute(value, both, [(flat(i, j), flat(i ^ half, j)) for i, j in group])
        row = [hidden[i * cut : (i + 1) * cut] for i in range(4)]
        across = lambda value: lax.ppermute(value, both, [(flat(i, j), flat(i, 1 - j)) for i, j in even])
        direct = [over(row[0], odd), over(row[2], odd)]
        swapped = [xor_permute(row[1], "head", 1), xor_permute(row[3], "head", 1)]
        key_half = xor_permute(local_key, "seq", half)
        w0 = start_weights(0, 1)
        w1 = start_weights(1, 2)
        w2 = start_weights(2, 4)
        step_rest = over_half(step_t)
        swapped[0] = order.wait(swapped[0])
        relayed = [over(swapped[0], even), None]
        swapped[1] = order.wait(swapped[1])
        relayed[1] = over(swapped[1], even)
        moved = [across(order.gate(row[0])), None]
        w0 = spread(order.wait(w0), "groups")

        def swap(i):
            got = order.wait((direct[i], relayed[i]))
            first = jnp.where(level, got[0], got[1])
            return first, xor_permute(first, "head", 1)

        def join(first, second):
            second = order.wait(second)
            return jnp.concatenate([jnp.where(level, first, second), jnp.where(level, second, first)], axis=0)

        first0, second0 = swap(0)
        moved[0] = order.wait(moved[0])
        moved[1] = across(order.gate(row[2]))
        w0 = spread(order.wait(w0), "batch")
        w1 = spread(order.wait(w1), "groups")
        others = [join(first0, second0)]
        weights.append((0, 1, order.wait(w0)))
        early = send(partial([([others[0]], BF16)], 0)[0])
        first1, second1 = swap(1)
        moved[1] = order.wait(moved[1])
        w1 = spread(order.wait(w1), "batch")
        mine = order.wait(
            jnp.where(level, hidden, jnp.concatenate([moved[0], swapped[0], moved[1], swapped[1]], axis=0))
        )
        key_half = order.wait(key_half)
        key_pair = jnp.concatenate([local_key, key_half], axis=0)
        key_rest = over_half(key_pair)
        step_rest = order.wait(step_rest)
        others.append(join(first1, second1))

    else:
        full = lax.all_gather(hidden, "head", axis=1, tiled=True)
        span_half = full.shape[1] // 2
        share = tokens // sides
        mine = lax.dynamic_slice_in_dim(full, side * span_half, span_half, 1)
        leaving = lax.dynamic_slice(full, (x * share, (1 - side) * span_half), (share, span_half))
        came = lax.all_gather(xor_permute(leaving, "seq", half), "head", axis=0, tiled=True)
        others = [came[: tokens // 2], came[tokens // 2 :]]
        key_pair = jnp.concatenate([local_key, xor_permute(local_key, "seq", half)], axis=0)
        step_rest = over_half(step_t)
        weights.append((0, 1, spread(spread(start_weights(0, 1), "groups"), "batch")))
        w1 = spread(spread(start_weights(1, 2), "groups"), "batch")
        w2 = start_weights(2, 4)
        key_rest = over_half(key_pair)
        early = send(partial([([others[0]], BF16)], 0)[0])

    extra_out = [
        jax.ShapeDtypeStruct((2 * tokens, width_b), F32),
        jax.ShapeDtypeStruct((2 * tokens, width_b), BF16),
        jax.ShapeDtypeStruct((padded, 2 * tokens), F32),
    ]
    extra_cols = [g[:, chunk:] for g in weights[0][2]]
    acts = (mine, *others)
    full, rounded, raw = order.wait(
        call(
            functools.partial(extra_kernel, model, list(range(half))),
            (order.gate(place), *acts, local_b, *extra_cols, step_t, *step_rest),
            [smem()]
            + [whole(a.shape) for a in acts]
            + [whole(local_b.shape)]
            + [whole((part, width_b))] * len(model)
            + [whole(step_t.shape)] * half,
            extra_out,
            "extra",
        )
    )
    came = send(rounded)
    came_raw = send(raw)
    w2 = spread(order.wait(w2), "groups")
    kept, arrived, norms = [], [], []
    early = order.wait(early)
    leaving, stays = partial([([others[1]], BF16), ([mine], F32)], 0)
    arrived.append([early, send(leaving)])
    kept.append(stays)

    def full_partial(j):
        leaving, stays = partial([(others, BF16), ([mine], F32)], j)
        arrived.append([send(leaving)])
        kept.append(stays)

    weights.append((1, 2, order.wait(w1)))
    full_partial(1)
    key_rest = order.wait(key_rest)
    keys = jnp.concatenate([key_pair] + key_rest, axis=0)
    norms.append(order.wait(teacher(0, heads)))
    w2 = spread(order.wait(w2), "batch")
    came, came_raw = order.wait((came, came_raw))
    came = came.astype(F32)
    inputs_pair = (full + jnp.concatenate([came[tokens:], came[:tokens]], axis=0)).astype(BF16)
    raw_pair = raw + jnp.concatenate([came_raw[:, tokens:], came_raw[:, :tokens]], axis=1)
    inputs_rest = over_half(inputs_pair)
    raw_rest = over_half(raw_pair)
    norms.append(order.wait(teacher(heads, heads)))
    arrived[0] = order.wait(arrived[0])
    weights.append((2, 4, order.wait(w2)))
    full_partial(2)
    norms.append(order.wait(teacher(2 * heads, heads)))
    arrived[1] = order.wait(arrived[1])
    full_partial(3)
    norms.append(order.wait(teacher(3 * heads, heads)))
    inputs_rest, raw_rest = order.wait((inputs_rest, raw_rest))
    inputs = jnp.concatenate([inputs_pair] + inputs_rest, axis=0)
    raw_all = jnp.stack([r[:, i * tokens : (i + 1) * tokens] for r in [raw_pair] + raw_rest for i in range(2)])
    rate = jnp.pad(decay_rate, (0, padded - head_count))[:, None]
    factor, log_row, log_col, gain_col = call(
        functools.partial(decay_kernel, offsets),
        (order.gate(place), raw_all, rate),
        [smem(), whole(raw_all.shape), whole(rate.shape)],
        [
            jax.ShapeDtypeStruct((padded, span), F32),
            jax.ShapeDtypeStruct((padded, tokens), F32),
            jax.ShapeDtypeStruct((tokens, 128), F32),
            jax.ShapeDtypeStruct((tokens, 128), F32),
        ],
        "decay",
    )
    factor = order.wait(factor)

    losses = []
    for j in range(count):
        group = j * heads // per_group
        came = order.wait(arrived[j])
        losses.append(
            order.wait(
                call(
                    functools.partial(loss_kernel, offsets, j * heads, heads),
                    (place, query, kept[j], keys, inputs, norms[j], factor, log_row, log_col, gain_col, *came),
                    [
                        smem(),
                        columns(tokens, chunk, j),
                        whole((tokens, chunk)),
                        columns(span, HEAD_DIM, group),
                        columns(span, HEAD_DIM, group),
                        whole(norms[j].shape),
                        whole(factor.shape),
                        whole(log_row.shape),
                        whole(log_col.shape),
                        whole(gain_col.shape),
                    ]
                    + [whole(c.shape) for c in came],
                    [jax.ShapeDtypeStruct((heads, 1, tokens), F32)],
                    "loss",
                )[0]
            )
        )
    return jnp.concatenate(losses, axis=0).reshape(1, head_count, tokens)


def solution(mesh):
    in_specs = (
        P(("groups", "batch"), "seq", "head"),
        P(("groups", "batch"), "seq", "head"),
        P(("groups", "batch"), "seq", None),
        P("seq", "head"),
        P("seq", None),
        P("seq", "head"),
        P("head"),
    )
    out_specs = P(("groups", "batch"), "head", "seq")
    return jax.shard_map(local, mesh=mesh, in_specs=in_specs, out_specs=out_specs, check_vma=False)
```

```python
import functools
import math

import jax
import jax.numpy as jnp
from jax import lax
from jax.experimental import pallas as pl
from jax.experimental.pallas import tpu as pltpu
from jax.sharding import PartitionSpec as P

HEADS = 32
KV_HEADS = 4
HEAD_DIM = 128
LOG2E = math.log2(math.e)
BF16 = jnp.bfloat16
F32 = jnp.float32
VMEM_LIMIT = 48 * 1024 * 1024

NT = (((1,), (1,)), ((), ()))


def xor_permute(value, axis, offset):
    size = lax.axis_size(axis)
    return lax.ppermute(value, axis, [(i, i ^ offset) for i in range(size)])


def whole(shape):
    return pl.BlockSpec(shape, lambda *_: (0,) * len(shape))


def columns(rows, width, index):
    return pl.BlockSpec((rows, width), lambda *_: (0, index))


def smem():
    return pl.BlockSpec(memory_space=pltpu.SMEM)


def call(kernel, args, in_specs, out_shapes, name, scratch=()):
    return pl.pallas_call(
        kernel,
        grid=(1,),
        in_specs=in_specs,
        out_specs=tuple(whole(s.shape) for s in out_shapes),
        out_shape=tuple(out_shapes),
        scratch_shapes=list(scratch),
        compiler_params=pltpu.CompilerParams(vmem_limit_bytes=VMEM_LIMIT),
        name=name,
    )(*args)


def product(place, act, own, pieces, model):
    block, quarter = place[0], place[1]
    rows = own.shape[0]
    total = jnp.dot(
        act[:, pl.ds(pl.multiple_of(block * rows, rows), rows)], own[...], preferred_element_type=F32
    )
    for piece, (step, turn) in zip(pieces, model):
        part = piece.shape[0]
        start = (block ^ step) * rows + (quarter ^ turn) * part
        total += jnp.dot(
            act[:, pl.ds(pl.multiple_of(start, part), part)], piece[...], preferred_element_type=F32
        )
    return total


def partial_kernel(model, groups, place, *rest):
    number = sum(groups)
    acts, own, pieces, outs = rest[:number], rest[number], rest[number + 1 : -len(groups)], rest[-len(groups) :]
    acts = list(acts)
    for size, out in zip(groups, outs):
        row = 0
        for act in acts[:size]:
            out[row : row + act.shape[0], :] = product(place, act, own, pieces, model).astype(out.dtype)
            row += act.shape[0]
        del acts[:size]


def pack_raw(raw, out):
    heads, tokens = raw.shape
    width = out.shape[1]
    row = tokens
    for first in range(0, tokens, width):
        value = raw[:, first : first + width]
        high = value.astype(BF16)
        out[row : row + heads, :] = high
        out[row + heads : row + 2 * heads, :] = (value - high.astype(F32)).astype(BF16)
        row += 2 * heads


def unpack_raw(packed, tokens, heads):
    width = packed.shape[1]
    parts = []
    row = tokens
    for _ in range(0, tokens, width):
        parts.append(packed[row : row + heads, :].astype(F32) + packed[row + heads : row + 2 * heads, :].astype(F32))
        row += 2 * heads
    return jnp.concatenate(parts, axis=1)


def extra_kernel(model, step_model, place, act_own, act_low, act_high, own, *rest):
    n = len(model)
    pieces = rest[:n]
    step_pieces = rest[n : n + len(step_model)]
    full, raw, packed = rest[-3:]
    first = 0
    for act in (act_own, act_low, act_high):
        here = slice(first, first + act.shape[0])
        first += act.shape[0]
        value = product(place, act, own, pieces, model)
        full[here, :] = value
        packed[here, :] = value.astype(BF16)
        total = None
        for piece, step in zip(step_pieces, step_model):
            rows = piece.shape[1]
            start = pl.multiple_of((place[0] ^ step) * rows, rows)
            part = lax.dot_general(piece[...], act[:, pl.ds(start, rows)], NT, preferred_element_type=F32)
            total = part if total is None else total + part
        raw[:, here] = total
    pack_raw(raw[...], packed)


def combine_kernel(full, raw, came, out):
    heads, tokens = raw.shape
    half = tokens // 2
    for a, b in ((0, half), (half, 0)):
        out[a : a + half, :] = (full[a : a + half, :] + came[b : b + half, :].astype(F32)).astype(BF16)
    other = unpack_raw(came, tokens, heads)
    pack_raw(raw[...] + jnp.concatenate([other[:, half:], other[:, :half]], axis=1), out)


def decay_kernel(offsets, tokens, place, rate, *rest):
    packed = rest[:-4]
    factor, log_row, log_col, gain_col = rest[-4:]
    mine = place[2]
    heads = rate.shape[0]
    pairs = [unpack_raw(p, 2 * tokens, heads) for p in packed]
    lane = lax.broadcasted_iota(jnp.int32, (heads, tokens), 1)
    steps, logs, totals = [], [], []
    for at in range(len(offsets)):
        value = pairs[at // 2][:, at % 2 * tokens : (at % 2 + 1) * tokens]
        step = jnp.maximum(value, 0.0) + jnp.log1p(jnp.exp(-jnp.abs(value)))
        log = step * (-LOG2E * rate[...])
        shift = 1
        while shift < tokens:
            log = log + jnp.where(lane >= shift, pltpu.roll(log, shift, 1), 0.0)
            shift *= 2
        steps.append(step)
        logs.append(log)
        totals.append(log[:, tokens - 1 :])
    for at, offset in enumerate(offsets):
        here = slice(at * tokens, (at + 1) * tokens)
        if at == 0:
            factor[:, here] = steps[0]
            continue
        between = jnp.zeros_like(totals[0])
        first = mine ^ offset
        for other, distance in enumerate(offsets):
            block = mine ^ distance
            inside = jnp.logical_and(block > first, block < mine)
            between += jnp.where(inside, totals[other], 0.0)
        factor[:, here] = steps[at] * jnp.exp2(totals[at] - logs[at] + between)
    log_row[...] = logs[0]
    wide = jnp.concatenate([logs[0], jnp.zeros((128 - heads, tokens), F32)], axis=0)
    turned = wide.T
    log_col[...] = turned
    gain_col[...] = jnp.exp2(turned)


def causal_of(tokens):
    row = lax.broadcasted_iota(jnp.int32, (tokens, tokens), 0)
    col = lax.broadcasted_iota(jnp.int32, (tokens, tokens), 1)
    return col <= row


def folded(combine, value):
    parts = [value[:, i : i + 128] for i in range(0, value.shape[1], 128)]
    return functools.reduce(combine, parts)


SCALE = LOG2E * HEAD_DIM ** -0.5


def for_place(mine, offsets, body):
    for position in range(len(offsets)):
        earlier = [at for at in range(1, len(offsets)) if (position ^ offsets[at]) < position]
        pl.when(mine == position)(functools.partial(body, earlier))


def teacher_kernel(offsets, place, query, *rest):
    keys, norm = rest[:-1], rest[-1]
    tokens = query.shape[0]

    def body(earlier):
        asked = query[...]
        scores = []
        for at in [0] + earlier:
            key = keys[at // 2][pl.ds(at % 2 * tokens, tokens), :]
            scores.append(lax.dot_general(asked, key, NT, preferred_element_type=F32) * SCALE)
        scores[0] = jnp.where(causal_of(tokens), scores[0], -jnp.inf)
        top = functools.reduce(jnp.maximum, [folded(jnp.maximum, s) for s in scores])
        peak = jnp.max(top, axis=1, keepdims=True)
        mass = functools.reduce(jnp.add, [folded(jnp.add, jnp.exp2(s - peak)) for s in scores])
        total = jnp.sum(mass, axis=1, keepdims=True)
        norm[0] = jnp.broadcast_to(peak + jnp.log2(total), (tokens, 128))

    for_place(place[2], offsets, body)


def loss_kernel(
    offsets, first, heads, number, place, query, kept, norm, factor, log_row, log_col, gain_col, *rest
):
    arrived, rest, out = rest[:number], rest[number:-1], rest[-1]
    keys, inputs = rest[: len(rest) // 2], rest[len(rest) // 2 :]
    tokens = query.shape[0]

    lane = lax.broadcasted_iota(jnp.int32, (tokens, 128), 1)

    def body(earlier):
        def one_head(i, carry):
            head = first + i
            cols = pl.ds(pl.multiple_of(i * HEAD_DIM, HEAD_DIM), HEAD_DIM)

            def column(ref):
                return jnp.sum(jnp.where(lane == head, ref[...], 0.0), axis=1, keepdims=True)

            asked = query[:, cols]
            came = jnp.concatenate([a[:, cols] for a in arrived], axis=0)
            read = (kept[:, cols] + came.astype(F32)).astype(BF16)
            lse = jnp.concatenate([norm[i]] * (tokens // 128), axis=1)
            gain = column(gain_col)
            sums = None
            for at in [0] + earlier:
                rows = pl.ds(at % 2 * tokens, tokens)
                score = lax.dot_general(asked, keys[at // 2][rows, :], NT, preferred_element_type=F32) * SCALE
                inner = lax.dot_general(read, inputs[at // 2][rows, :], NT, preferred_element_type=F32)
                inner = inner * factor[pl.ds(head, 1), at * tokens : (at + 1) * tokens]
                prob = jnp.exp2(score - lse)
                if at == 0:
                    gap = column(log_col) - log_row[pl.ds(head, 1), :]
                    diff = jnp.where(causal_of(tokens), prob - inner * jnp.exp2(gap), 0.0)
                else:
                    diff = prob - inner * gain
                square = folded(jnp.add, diff * diff)
                sums = square if sums is None else sums + square
            out[i] = jnp.sum(sums.T, axis=0, keepdims=True)
            return carry

        lax.fori_loop(0, heads, one_head, 0, unroll=2 if heads % 2 == 0 else 1)

    for_place(place[2], offsets, body)


class Order:
    def __init__(self):
        self.last = ()

    def gate(self, value):
        if not self.last:
            return value
        value, self.last = lax.optimization_barrier((value, self.last))
        return value

    def wait(self, value):
        value, _ = lax.optimization_barrier((value, self.last))
        self.last = tuple(jax.tree.leaves(value))
        return value


def xor_sums(offset_size, scale):
    got = [0]
    d = 1
    while d < offset_size:
        got += [g ^ (d * scale) for g in got]
        d *= 2
    return got


def spread(pieces, axis):
    got = list(pieces)
    d = 1
    while d < lax.axis_size(axis):
        got += [xor_permute(g, axis, d) for g in got]
        d *= 2
    return got


def local(hidden_in, teacher_query, teacher_key, proj_c, proj_b, proj_step, decay_rate):
    _, tokens, _ = hidden_in.shape
    hidden = hidden_in[0]
    rows, width = proj_c.shape
    head_count = proj_step.shape[1]
    seq, sides = lax.axis_size("seq"), lax.axis_size("head")
    half = seq // 2
    copies_y, copies_c = lax.axis_size("groups"), lax.axis_size("batch")
    copies = copies_y * copies_c
    z, x = lax.axis_index("seq"), lax.axis_index("head")
    side = z // half
    quarter = lax.axis_index("groups") * copies_c + lax.axis_index("batch")
    place = jnp.stack([z % half, quarter, z]).astype(jnp.int32)
    per_model_group = HEADS // KV_HEADS
    group_count = max(1, head_count // per_model_group)
    per_group = head_count // group_count
    group_first = x * head_count // per_model_group
    width_b = group_count * HEAD_DIM
    offsets = [0, half]
    for d in range(1, half):
        offsets += [d, d ^ half]
    padded = max(16, head_count)
    span = seq * tokens
    chunk = max(HEAD_DIM, width // 4)
    count = width // chunk
    heads = chunk // HEAD_DIM
    part = rows // copies
    turns = xor_sums(copies_y, copies_c)
    turns = [t ^ c for c in xor_sums(copies_c, 1) for t in turns]
    model = [(d, t) for d in range(1, half) for t in turns]
    query = teacher_query[0]
    order = Order()

    def over_half(value):
        return [xor_permute(value, "seq", d) for d in range(1, half)]

    def start_weights(first, last):
        piece = lax.dynamic_slice(proj_c, (quarter * part, first * chunk), (part, (last - first) * chunk))
        if first == 0:
            extra = lax.dynamic_slice(proj_b, (quarter * part, group_first * HEAD_DIM), (part, width_b))
            piece = jnp.concatenate([piece, extra], axis=1)
        return over_half(piece)

    def send(value):
        return xor_permute(value, "seq", half)

    def partial(acts, j):
        first, _, pieces = next(w for w in weights if w[0] <= j < w[1])
        flat_acts = [a for blocks, _ in acts for a in blocks]
        return order.wait(
            call(
                functools.partial(partial_kernel, model, [len(blocks) for blocks, _ in acts]),
                (order.gate(place), *flat_acts, proj_c, *pieces),
                [smem()]
                + [whole(a.shape) for a in flat_acts]
                + [columns(rows, chunk, j)]
                + [columns(part, chunk, j - first)] * len(model),
                [jax.ShapeDtypeStruct((sum(a.shape[0] for a in blocks), chunk), dtype) for blocks, dtype in acts],
                "partial",
            )
        )

    def teacher(first, number):
        return pl.pallas_call(
            functools.partial(teacher_kernel, offsets),
            grid=(number,),
            in_specs=[
                smem(),
                pl.BlockSpec((tokens, HEAD_DIM), lambda h: (0, first + h)),
            ]
            + [pl.BlockSpec((2 * tokens, HEAD_DIM), lambda h: (0, (first + h) // per_group))] * half,
            out_specs=pl.BlockSpec((1, tokens, 128), lambda h: (h, 0, 0)),
            out_shape=jax.ShapeDtypeStruct((number, tokens, 128), F32),
            compiler_params=pltpu.CompilerParams(vmem_limit_bytes=VMEM_LIMIT),
            name="teacher",
        )(order.gate(place), query, *keys)

    spans = [(0, 1), (1, 2), (2, 4)]
    weights = []
    local_key = lax.dynamic_slice_in_dim(teacher_key[0], group_first * HEAD_DIM, width_b, 1)
    local_b = lax.dynamic_slice_in_dim(proj_b, group_first * HEAD_DIM, width_b, 1)
    step_t = jnp.pad(proj_step.T, ((0, padded - head_count), (0, 0)))

    if sides == 2:
        cut = tokens // 4
        spots = [(i, j) for i in range(seq) for j in range(2)]
        flat = lambda i, j: i * 2 + j
        both = ("seq", "head")
        level = side == x
        even = [s for s in spots if s[0] // half == s[1]]
        odd = [s for s in spots if s[0] // half != s[1]]
        over = lambda value, group: lax.ppermute(value, both, [(flat(i, j), flat(i ^ half, j)) for i, j in group])
        row = [hidden[i * cut : (i + 1) * cut] for i in range(4)]
        across = lambda value: lax.ppermute(value, both, [(flat(i, j), flat(i, 1 - j)) for i, j in even])
        direct = [over(row[0], odd), over(row[2], odd)]
        swapped = [xor_permute(row[1], "head", 1), xor_permute(row[3], "head", 1)]
        key_half = xor_permute(local_key, "seq", half)
        w0 = start_weights(0, 1)
        w1 = start_weights(1, 2)
        w2 = start_weights(2, 4)
        step_rest = over_half(step_t)
        swapped[0] = order.wait(swapped[0])
        relayed = [over(swapped[0], even), None]
        swapped[1] = order.wait(swapped[1])
        relayed[1] = over(swapped[1], even)
        moved = [across(order.gate(row[0])), None]
        w0 = spread(order.wait(w0), "groups")

        def swap(i):
            got = order.wait((direct[i], relayed[i]))
            first = jnp.where(level, got[0], got[1])
            return first, xor_permute(first, "head", 1)

        def join(first, second):
            second = order.wait(second)
            return jnp.concatenate([jnp.where(level, first, second), jnp.where(level, second, first)], axis=0)

        first0, second0 = swap(0)
        moved[0] = order.wait(moved[0])
        moved[1] = across(order.gate(row[2]))
        w0 = spread(order.wait(w0), "batch")
        w1 = spread(order.wait(w1), "groups")
        others = [join(first0, second0)]
        weights.append((0, 1, order.wait(w0)))
        first1, second1 = swap(1)
        moved[1] = order.wait(moved[1])
        w1 = spread(order.wait(w1), "batch")
        mine = order.wait(
            jnp.where(level, hidden, jnp.concatenate([moved[0], swapped[0], moved[1], swapped[1]], axis=0))
        )
        key_half = order.wait(key_half)
        key_pair = jnp.concatenate([local_key, key_half], axis=0)
        key_rest = over_half(key_pair)
        step_rest = order.wait(step_rest)
        others.append(join(first1, second1))

    else:
        full = lax.all_gather(hidden, "head", axis=1, tiled=True)
        span_half = full.shape[1] // 2
        share = tokens // sides
        mine = lax.dynamic_slice_in_dim(full, side * span_half, span_half, 1)
        leaving = lax.dynamic_slice(full, (x * share, (1 - side) * span_half), (share, span_half))
        came = lax.all_gather(xor_permute(leaving, "seq", half), "head", axis=0, tiled=True)
        others = [came[: tokens // 2], came[tokens // 2 :]]
        key_pair = jnp.concatenate([local_key, xor_permute(local_key, "seq", half)], axis=0)
        step_rest = over_half(step_t)
        weights.append((0, 1, spread(spread(start_weights(0, 1), "groups"), "batch")))
        w1 = spread(spread(start_weights(1, 2), "groups"), "batch")
        w2 = start_weights(2, 4)
        key_rest = over_half(key_pair)

    packed_rows = 2 * tokens + 2 * padded * (2 * tokens // width_b)
    packed_shape = jax.ShapeDtypeStruct((packed_rows, width_b), BF16)
    extra_out = [
        jax.ShapeDtypeStruct((2 * tokens, width_b), F32),
        jax.ShapeDtypeStruct((padded, 2 * tokens), F32),
        packed_shape,
    ]
    acts = (mine, *others)
    full, raw, packed = order.wait(
        call(
            functools.partial(extra_kernel, model, list(range(half))),
            (order.gate(place), *acts, local_b, *weights[0][2], step_t, *step_rest),
            [smem()]
            + [whole(a.shape) for a in acts]
            + [whole(local_b.shape)]
            + [columns(part, width_b, chunk // width_b)] * len(model)
            + [whole(step_t.shape)] * half,
            extra_out,
            "extra",
        )
    )
    came = send(packed)
    w2 = spread(order.wait(w2), "groups")
    kept, arrived, norms = [], [], []
    def full_partial(j):
        leaving, stays = partial([(others, BF16), ([mine], F32)], j)
        arrived.append([send(leaving)])
        kept.append(stays)

    full_partial(0)
    weights.append((1, 2, order.wait(w1)))
    full_partial(1)
    came = order.wait(came)
    pair = order.wait(
        call(
            combine_kernel,
            (full, raw, came),
            [whole(full.shape), whole(raw.shape), whole(came.shape)],
            [packed_shape],
            "combine",
        )[0]
    )
    pair_rest = over_half(pair)
    key_rest = order.wait(key_rest)
    keys = [key_pair] + key_rest
    arrived[0] = order.wait(arrived[0])
    norms.append(order.wait(teacher(0, heads)))
    w2 = spread(order.wait(w2), "batch")
    norms.append(order.wait(teacher(heads, heads)))
    weights.append((2, 4, order.wait(w2)))
    full_partial(2)
    norms.append(order.wait(teacher(2 * heads, heads)))
    arrived[1] = order.wait(arrived[1])
    full_partial(3)
    norms.append(order.wait(teacher(3 * heads, heads)))
    inputs = [pair] + order.wait(pair_rest)
    rate = jnp.pad(decay_rate, (0, padded - head_count))[:, None]
    factor, log_row, log_col, gain_col = call(
        functools.partial(decay_kernel, offsets, tokens),
        (order.gate(place), rate, *inputs),
        [smem(), whole(rate.shape)] + [whole(packed_shape.shape)] * half,
        [
            jax.ShapeDtypeStruct((padded, span), F32),
            jax.ShapeDtypeStruct((padded, tokens), F32),
            jax.ShapeDtypeStruct((tokens, 128), F32),
            jax.ShapeDtypeStruct((tokens, 128), F32),
        ],
        "decay",
    )
    factor = order.wait(factor)

    losses = []
    for j in range(count):
        group = j * heads // per_group
        came = order.wait(arrived[j])
        losses.append(
            order.wait(
                call(
                    functools.partial(loss_kernel, offsets, j * heads, heads, len(came)),
                    (place, query, kept[j], norms[j], factor, log_row, log_col, gain_col, *came, *keys, *inputs),
                    [
                        smem(),
                        columns(tokens, chunk, j),
                        whole((tokens, chunk)),
                        whole(norms[j].shape),
                        whole(factor.shape),
                        whole(log_row.shape),
                        whole(log_col.shape),
                        whole(gain_col.shape),
                    ]
                    + [whole(c.shape) for c in came]
                    + [columns(2 * tokens, HEAD_DIM, group)] * (2 * half),
                    [jax.ShapeDtypeStruct((heads, 1, tokens), F32)],
                    "loss",
                )[0]
            )
        )
    return jnp.concatenate(losses, axis=0).reshape(1, head_count, tokens)


def solution(mesh):
    in_specs = (
        P(("groups", "batch"), "seq", "head"),
        P(("groups", "batch"), "seq", "head"),
        P(("groups", "batch"), "seq", None),
        P("seq", "head"),
        P("seq", None),
        P("seq", "head"),
        P("head"),
    )
    out_specs = P(("groups", "batch"), "head", "seq")
    return jax.shard_map(local, mesh=mesh, in_specs=in_specs, out_specs=out_specs, check_vma=False)
```

```python
import functools
import math

import jax
import jax.numpy as jnp
from jax import lax
from jax.experimental import pallas as pl
from jax.experimental.pallas import tpu as pltpu
from jax.sharding import PartitionSpec as P

HEADS = 32
KV_HEADS = 4
HEAD_DIM = 128
LOG2E = math.log2(math.e)
BF16 = jnp.bfloat16
F32 = jnp.float32
VMEM_LIMIT = 48 * 1024 * 1024

NT = (((1,), (1,)), ((), ()))


def xor_permute(value, axis, offset):
    size = lax.axis_size(axis)
    return lax.ppermute(value, axis, [(i, i ^ offset) for i in range(size)])


def whole(shape):
    return pl.BlockSpec(shape, lambda *_: (0,) * len(shape))


def columns(rows, width, index):
    return pl.BlockSpec((rows, width), lambda *_: (0, index))


def smem():
    return pl.BlockSpec(memory_space=pltpu.SMEM)


def call(kernel, args, in_specs, out_shapes, name, scratch=()):
    return pl.pallas_call(
        kernel,
        grid=(1,),
        in_specs=in_specs,
        out_specs=tuple(whole(s.shape) for s in out_shapes),
        out_shape=tuple(out_shapes),
        scratch_shapes=list(scratch),
        compiler_params=pltpu.CompilerParams(vmem_limit_bytes=VMEM_LIMIT),
        name=name,
    )(*args)


def product(place, act, own, pieces, model):
    block, quarter = place[0], place[1]
    rows = own.shape[0]
    total = jnp.dot(
        act[:, pl.ds(pl.multiple_of(block * rows, rows), rows)], own[...], preferred_element_type=F32
    )
    for piece, (step, turn) in zip(pieces, model):
        part = piece.shape[0]
        start = (block ^ step) * rows + (quarter ^ turn) * part
        total += jnp.dot(
            act[:, pl.ds(pl.multiple_of(start, part), part)], piece[...], preferred_element_type=F32
        )
    return total


def partial_kernel(model, groups, place, *rest):
    number = sum(groups)
    acts, own, pieces, outs = rest[:number], rest[number], rest[number + 1 : -len(groups)], rest[-len(groups) :]
    acts = list(acts)
    for size, out in zip(groups, outs):
        row = 0
        for act in acts[:size]:
            out[row : row + act.shape[0], :] = product(place, act, own, pieces, model).astype(out.dtype)
            row += act.shape[0]
        del acts[:size]


def pack_raw(raw, out):
    heads, tokens = raw.shape
    width = out.shape[1]
    row = tokens
    for first in range(0, tokens, width):
        value = raw[:, first : first + width]
        high = value.astype(BF16)
        out[row : row + heads, :] = high
        out[row + heads : row + 2 * heads, :] = (value - high.astype(F32)).astype(BF16)
        row += 2 * heads


def unpack_raw(packed, tokens, heads):
    width = packed.shape[1]
    parts = []
    row = tokens
    for _ in range(0, tokens, width):
        parts.append(packed[row : row + heads, :].astype(F32) + packed[row + heads : row + 2 * heads, :].astype(F32))
        row += 2 * heads
    return jnp.concatenate(parts, axis=1)


def extra_kernel(model, step_model, place, act_own, act_low, act_high, own, *rest):
    n = len(model)
    pieces = rest[:n]
    step_pieces = rest[n : n + len(step_model)]
    full, raw, packed = rest[-3:]
    first = 0
    for act in (act_own, act_low, act_high):
        here = slice(first, first + act.shape[0])
        first += act.shape[0]
        value = product(place, act, own, pieces, model)
        full[here, :] = value
        packed[here, :] = value.astype(BF16)
        total = None
        for piece, step in zip(step_pieces, step_model):
            rows = piece.shape[1]
            start = pl.multiple_of((place[0] ^ step) * rows, rows)
            part = lax.dot_general(piece[...], act[:, pl.ds(start, rows)], NT, preferred_element_type=F32)
            total = part if total is None else total + part
        raw[:, here] = total
    pack_raw(raw[...], packed)


def combine_kernel(full, raw, came, out):
    heads, tokens = raw.shape
    half = tokens // 2
    for a, b in ((0, half), (half, 0)):
        out[a : a + half, :] = (full[a : a + half, :] + came[b : b + half, :].astype(F32)).astype(BF16)
    other = unpack_raw(came, tokens, heads)
    pack_raw(raw[...] + jnp.concatenate([other[:, half:], other[:, :half]], axis=1), out)


def decay_kernel(offsets, tokens, place, rate, *rest):
    packed = rest[:-4]
    factor, log_row, log_col, gain_col = rest[-4:]
    mine = place[2]
    heads = rate.shape[0]
    pairs = [unpack_raw(p, 2 * tokens, heads) for p in packed]
    lane = lax.broadcasted_iota(jnp.int32, (heads, tokens), 1)
    steps, logs, totals = [], [], []
    for at in range(len(offsets)):
        value = pairs[at // 2][:, at % 2 * tokens : (at % 2 + 1) * tokens]
        step = jnp.maximum(value, 0.0) + jnp.log1p(jnp.exp(-jnp.abs(value)))
        log = step * (-LOG2E * rate[...])
        shift = 1
        while shift < tokens:
            log = log + jnp.where(lane >= shift, pltpu.roll(log, shift, 1), 0.0)
            shift *= 2
        steps.append(step)
        logs.append(log)
        totals.append(log[:, tokens - 1 :])
    for at, offset in enumerate(offsets):
        here = slice(at * tokens, (at + 1) * tokens)
        if at == 0:
            factor[:, here] = steps[0]
            continue
        between = jnp.zeros_like(totals[0])
        first = mine ^ offset
        for other, distance in enumerate(offsets):
            block = mine ^ distance
            inside = jnp.logical_and(block > first, block < mine)
            between += jnp.where(inside, totals[other], 0.0)
        factor[:, here] = steps[at] * jnp.exp2(totals[at] - logs[at] + between)
    log_row[...] = logs[0]
    wide = jnp.concatenate([logs[0], jnp.zeros((128 - heads, tokens), F32)], axis=0)
    turned = wide.T
    log_col[...] = turned
    gain_col[...] = jnp.exp2(turned)


def causal_of(tokens):
    row = lax.broadcasted_iota(jnp.int32, (tokens, tokens), 0)
    col = lax.broadcasted_iota(jnp.int32, (tokens, tokens), 1)
    return col <= row


def folded(combine, value):
    parts = [value[:, i : i + 128] for i in range(0, value.shape[1], 128)]
    return functools.reduce(combine, parts)


SCALE = LOG2E * HEAD_DIM ** -0.5


def for_place(mine, offsets, body):
    for position in range(len(offsets)):
        earlier = [at for at in range(1, len(offsets)) if (position ^ offsets[at]) < position]
        pl.when(mine == position)(functools.partial(body, earlier))


def teacher_kernel(offsets, place, query, *rest):
    keys, norm = rest[:-1], rest[-1]
    tokens = query.shape[0]

    def body(earlier):
        asked = query[...]
        scores = []
        for at in [0] + earlier:
            key = keys[at // 2][pl.ds(at % 2 * tokens, tokens), :]
            scores.append(lax.dot_general(asked, key, NT, preferred_element_type=F32) * SCALE)
        scores[0] = jnp.where(causal_of(tokens), scores[0], -jnp.inf)
        top = functools.reduce(jnp.maximum, [folded(jnp.maximum, s) for s in scores])
        peak = jnp.max(top, axis=1, keepdims=True)
        mass = functools.reduce(jnp.add, [folded(jnp.add, jnp.exp2(s - peak)) for s in scores])
        total = jnp.sum(mass, axis=1, keepdims=True)
        norm[0] = jnp.broadcast_to(peak + jnp.log2(total), (tokens, 128))

    for_place(place[2], offsets, body)


def loss_kernel(
    offsets, first, heads, number, place, query, kept, norm, factor, log_row, log_col, gain_col, *rest
):
    arrived, rest, out = rest[:number], rest[number:-1], rest[-1]
    keys, inputs = rest[: len(rest) // 2], rest[len(rest) // 2 :]
    tokens = query.shape[0]

    lane = lax.broadcasted_iota(jnp.int32, (tokens, 128), 1)

    def body(earlier):
        def one_head(i, carry):
            head = first + i
            cols = pl.ds(pl.multiple_of(i * HEAD_DIM, HEAD_DIM), HEAD_DIM)

            def column(ref):
                return jnp.sum(jnp.where(lane == head, ref[...], 0.0), axis=1, keepdims=True)

            asked = query[:, cols]
            came = jnp.concatenate([a[:, cols] for a in arrived], axis=0)
            read = (kept[:, cols] + came.astype(F32)).astype(BF16)
            lse = jnp.concatenate([norm[i]] * (tokens // 128), axis=1)
            gain = column(gain_col)
            sums = None
            for at in [0] + earlier:
                rows = pl.ds(at % 2 * tokens, tokens)
                score = lax.dot_general(asked, keys[at // 2][rows, :], NT, preferred_element_type=F32) * SCALE
                inner = lax.dot_general(read, inputs[at // 2][rows, :], NT, preferred_element_type=F32)
                inner = inner * factor[pl.ds(head, 1), at * tokens : (at + 1) * tokens]
                prob = jnp.exp2(score - lse)
                if at == 0:
                    gap = column(log_col) - log_row[pl.ds(head, 1), :]
                    diff = jnp.where(causal_of(tokens), prob - inner * jnp.exp2(gap), 0.0)
                else:
                    diff = prob - inner * gain
                square = folded(jnp.add, diff * diff)
                sums = square if sums is None else sums + square
            out[i] = jnp.sum(sums.T, axis=0, keepdims=True)
            return carry

        lax.fori_loop(0, heads, one_head, 0, unroll=2 if heads % 2 == 0 else 1)

    for_place(place[2], offsets, body)


class Order:
    def __init__(self):
        self.last = ()

    def gate(self, value):
        if not self.last:
            return value
        value, self.last = lax.optimization_barrier((value, self.last))
        return value

    def wait(self, value):
        value, _ = lax.optimization_barrier((value, self.last))
        self.last = tuple(jax.tree.leaves(value))
        return value


def xor_sums(offset_size, scale):
    got = [0]
    d = 1
    while d < offset_size:
        got += [g ^ (d * scale) for g in got]
        d *= 2
    return got


def spread(pieces, axis):
    got = list(pieces)
    d = 1
    while d < lax.axis_size(axis):
        got += [xor_permute(g, axis, d) for g in got]
        d *= 2
    return got


def local(hidden_in, teacher_query, teacher_key, proj_c, proj_b, proj_step, decay_rate):
    _, tokens, _ = hidden_in.shape
    hidden = hidden_in[0]
    rows, width = proj_c.shape
    head_count = proj_step.shape[1]
    seq, sides = lax.axis_size("seq"), lax.axis_size("head")
    half = seq // 2
    copies_y, copies_c = lax.axis_size("groups"), lax.axis_size("batch")
    copies = copies_y * copies_c
    z, x = lax.axis_index("seq"), lax.axis_index("head")
    side = z // half
    quarter = lax.axis_index("groups") * copies_c + lax.axis_index("batch")
    place = jnp.stack([z % half, quarter, z]).astype(jnp.int32)
    per_model_group = HEADS // KV_HEADS
    group_count = max(1, head_count // per_model_group)
    per_group = head_count // group_count
    group_first = x * head_count // per_model_group
    width_b = group_count * HEAD_DIM
    offsets = [0, half]
    for d in range(1, half):
        offsets += [d, d ^ half]
    padded = max(16, head_count)
    span = seq * tokens
    chunk = max(HEAD_DIM, width // 4)
    count = width // chunk
    heads = chunk // HEAD_DIM
    part = rows // copies
    turns = xor_sums(copies_y, copies_c)
    turns = [t ^ c for c in xor_sums(copies_c, 1) for t in turns]
    model = [(d, t) for d in range(1, half) for t in turns]
    query = teacher_query[0]
    order = Order()

    def over_half(value):
        return [xor_permute(value, "seq", d) for d in range(1, half)]

    def start_weights(first, last):
        piece = lax.dynamic_slice(proj_c, (quarter * part, first * chunk), (part, (last - first) * chunk))
        if first == 0:
            extra = lax.dynamic_slice(proj_b, (quarter * part, group_first * HEAD_DIM), (part, width_b))
            piece = jnp.concatenate([piece, extra], axis=1)
        return over_half(piece)

    def send(value):
        return xor_permute(value, "seq", half)

    def partial(acts, j):
        first, _, pieces = next(w for w in weights if w[0] <= j < w[1])
        flat_acts = [a for blocks, _ in acts for a in blocks]
        return order.wait(
            call(
                functools.partial(partial_kernel, model, [len(blocks) for blocks, _ in acts]),
                (order.gate(place), *flat_acts, proj_c, *pieces),
                [smem()]
                + [whole(a.shape) for a in flat_acts]
                + [columns(rows, chunk, j)]
                + [columns(part, chunk, j - first)] * len(model),
                [jax.ShapeDtypeStruct((sum(a.shape[0] for a in blocks), chunk), dtype) for blocks, dtype in acts],
                "partial",
            )
        )

    def teacher(first, number):
        return pl.pallas_call(
            functools.partial(teacher_kernel, offsets),
            grid=(number,),
            in_specs=[
                smem(),
                pl.BlockSpec((tokens, HEAD_DIM), lambda h: (0, first + h)),
            ]
            + [pl.BlockSpec((2 * tokens, HEAD_DIM), lambda h: (0, (first + h) // per_group))] * half,
            out_specs=pl.BlockSpec((1, tokens, 128), lambda h: (h, 0, 0)),
            out_shape=jax.ShapeDtypeStruct((number, tokens, 128), F32),
            compiler_params=pltpu.CompilerParams(vmem_limit_bytes=VMEM_LIMIT),
            name="teacher",
        )(order.gate(place), query, *keys)

    spans = [(0, 1), (1, 2), (2, 4)]
    weights = []
    local_key = lax.dynamic_slice_in_dim(teacher_key[0], group_first * HEAD_DIM, width_b, 1)
    local_b = lax.dynamic_slice_in_dim(proj_b, group_first * HEAD_DIM, width_b, 1)
    step_t = jnp.pad(proj_step.T, ((0, padded - head_count), (0, 0)))

    if sides == 2:
        cut = tokens // 4
        spots = [(i, j) for i in range(seq) for j in range(2)]
        flat = lambda i, j: i * 2 + j
        both = ("seq", "head")
        level = side == x
        even = [s for s in spots if s[0] // half == s[1]]
        odd = [s for s in spots if s[0] // half != s[1]]
        over = lambda value, group: lax.ppermute(value, both, [(flat(i, j), flat(i ^ half, j)) for i, j in group])
        row = [hidden[i * cut : (i + 1) * cut] for i in range(4)]
        across = lambda value: lax.ppermute(value, both, [(flat(i, j), flat(i, 1 - j)) for i, j in even])
        direct = [over(row[0], odd), over(row[2], odd)]
        swapped = [xor_permute(row[1], "head", 1), xor_permute(row[3], "head", 1)]
        key_half = xor_permute(local_key, "seq", half)
        w0 = start_weights(0, 1)
        w1 = start_weights(1, 2)
        w2 = start_weights(2, 4)
        step_rest = over_half(step_t)
        swapped[0] = order.wait(swapped[0])
        relayed = [over(swapped[0], even), None]
        swapped[1] = order.wait(swapped[1])
        relayed[1] = over(swapped[1], even)
        moved = [across(order.gate(row[0])), None]
        w0 = spread(order.wait(w0), "groups")

        def swap(i):
            got = order.wait((direct[i], relayed[i]))
            first = jnp.where(level, got[0], got[1])
            return first, xor_permute(first, "head", 1)

        def join(first, second):
            second = order.wait(second)
            return jnp.concatenate([jnp.where(level, first, second), jnp.where(level, second, first)], axis=0)

        first0, second0 = swap(0)
        moved[0] = order.wait(moved[0])
        moved[1] = across(order.gate(row[2]))
        w0 = spread(order.wait(w0), "batch")
        w1 = spread(order.wait(w1), "groups")
        others = [join(first0, second0)]
        weights.append((0, 1, order.wait(w0)))
        first1, second1 = swap(1)
        moved[1] = order.wait(moved[1])
        w1 = spread(order.wait(w1), "batch")
        mine = order.wait(
            jnp.where(level, hidden, jnp.concatenate([moved[0], swapped[0], moved[1], swapped[1]], axis=0))
        )
        key_half = order.wait(key_half)
        key_pair = jnp.concatenate([local_key, key_half], axis=0)
        key_rest = over_half(key_pair)
        step_rest = order.wait(step_rest)
        others.append(join(first1, second1))

    else:
        full = lax.all_gather(hidden, "head", axis=1, tiled=True)
        span_half = full.shape[1] // 2
        share = tokens // sides
        mine = lax.dynamic_slice_in_dim(full, side * span_half, span_half, 1)
        leaving = lax.dynamic_slice(full, (x * share, (1 - side) * span_half), (share, span_half))
        came = lax.all_gather(xor_permute(leaving, "seq", half), "head", axis=0, tiled=True)
        others = [came[: tokens // 2], came[tokens // 2 :]]
        key_pair = jnp.concatenate([local_key, xor_permute(local_key, "seq", half)], axis=0)
        step_rest = over_half(step_t)
        weights.append((0, 1, spread(spread(start_weights(0, 1), "groups"), "batch")))
        w1 = spread(spread(start_weights(1, 2), "groups"), "batch")
        w2 = start_weights(2, 4)
        key_rest = over_half(key_pair)

    packed_rows = 2 * tokens + 2 * padded * (2 * tokens // width_b)
    packed_shape = jax.ShapeDtypeStruct((packed_rows, width_b), BF16)
    extra_out = [
        jax.ShapeDtypeStruct((2 * tokens, width_b), F32),
        jax.ShapeDtypeStruct((padded, 2 * tokens), F32),
        packed_shape,
    ]
    acts = (mine, *others)
    full, raw, packed = order.wait(
        call(
            functools.partial(extra_kernel, model, list(range(half))),
            (order.gate(place), *acts, local_b, *weights[0][2], step_t, *step_rest),
            [smem()]
            + [whole(a.shape) for a in acts]
            + [whole(local_b.shape)]
            + [columns(part, width_b, chunk // width_b)] * len(model)
            + [whole(step_t.shape)] * half,
            extra_out,
            "extra",
        )
    )
    came = send(packed)
    w2 = spread(order.wait(w2), "groups")
    kept, arrived, norms = [], [], []
    def full_partial(j):
        leaving, stays = partial([(others, BF16), ([mine], F32)], j)
        arrived.append([send(leaving)])
        kept.append(stays)

    full_partial(0)
    weights.append((1, 2, order.wait(w1)))
    full_partial(1)
    came = order.wait(came)
    pair = order.wait(
        call(
            combine_kernel,
            (full, raw, came),
            [whole(full.shape), whole(raw.shape), whole(came.shape)],
            [packed_shape],
            "combine",
        )[0]
    )
    pair_rest = over_half(pair)
    key_rest = order.wait(key_rest)
    keys = [key_pair] + key_rest
    norms.append(order.wait(teacher(0, heads)))
    arrived[0] = order.wait(arrived[0])
    w2 = spread(order.wait(w2), "batch")
    norms.append(order.wait(teacher(heads, heads)))
    weights.append((2, 4, order.wait(w2)))
    full_partial(2)
    norms.append(order.wait(teacher(2 * heads, heads)))
    arrived[1] = order.wait(arrived[1])
    full_partial(3)
    norms.append(order.wait(teacher(3 * heads, heads)))
    inputs = [pair] + order.wait(pair_rest)
    rate = jnp.pad(decay_rate, (0, padded - head_count))[:, None]
    factor, log_row, log_col, gain_col = call(
        functools.partial(decay_kernel, offsets, tokens),
        (order.gate(place), rate, *inputs),
        [smem(), whole(rate.shape)] + [whole(packed_shape.shape)] * half,
        [
            jax.ShapeDtypeStruct((padded, span), F32),
            jax.ShapeDtypeStruct((padded, tokens), F32),
            jax.ShapeDtypeStruct((tokens, 128), F32),
            jax.ShapeDtypeStruct((tokens, 128), F32),
        ],
        "decay",
    )
    factor = order.wait(factor)

    losses = []
    for j in range(count):
        group = j * heads // per_group
        came = order.wait(arrived[j])
        losses.append(
            order.wait(
                call(
                    functools.partial(loss_kernel, offsets, j * heads, heads, len(came)),
                    (place, query, kept[j], norms[j], factor, log_row, log_col, gain_col, *came, *keys, *inputs),
                    [
                        smem(),
                        columns(tokens, chunk, j),
                        whole((tokens, chunk)),
                        whole(norms[j].shape),
                        whole(factor.shape),
                        whole(log_row.shape),
                        whole(log_col.shape),
                        whole(gain_col.shape),
                    ]
                    + [whole(c.shape) for c in came]
                    + [columns(2 * tokens, HEAD_DIM, group)] * (2 * half),
                    [jax.ShapeDtypeStruct((heads, 1, tokens), F32)],
                    "loss",
                )[0]
            )
        )
    return jnp.concatenate(losses, axis=0).reshape(1, head_count, tokens)


def solution(mesh):
    in_specs = (
        P(("groups", "batch"), "seq", "head"),
        P(("groups", "batch"), "seq", "head"),
        P(("groups", "batch"), "seq", None),
        P("seq", "head"),
        P("seq", None),
        P("seq", "head"),
        P("head"),
    )
    out_specs = P(("groups", "batch"), "head", "seq")
    return jax.shard_map(local, mesh=mesh, in_specs=in_specs, out_specs=out_specs, check_vma=False)
```

```python
import functools
import math

import jax
import jax.numpy as jnp
from jax import lax
from jax.experimental import pallas as pl
from jax.experimental.pallas import tpu as pltpu
from jax.sharding import PartitionSpec as P

HEADS = 32
KV_HEADS = 4
HEAD_DIM = 128
LOG2E = math.log2(math.e)
BF16 = jnp.bfloat16
F32 = jnp.float32
VMEM_LIMIT = 48 * 1024 * 1024

NT = (((1,), (1,)), ((), ()))


def xor_permute(value, axis, offset):
    size = lax.axis_size(axis)
    return lax.ppermute(value, axis, [(i, i ^ offset) for i in range(size)])


def whole(shape):
    return pl.BlockSpec(shape, lambda *_: (0,) * len(shape))


def columns(rows, width, index):
    return pl.BlockSpec((rows, width), lambda *_: (0, index))


def smem():
    return pl.BlockSpec(memory_space=pltpu.SMEM)


def call(kernel, args, in_specs, out_shapes, name, scratch=()):
    return pl.pallas_call(
        kernel,
        grid=(1,),
        in_specs=in_specs,
        out_specs=tuple(whole(s.shape) for s in out_shapes),
        out_shape=tuple(out_shapes),
        scratch_shapes=list(scratch),
        compiler_params=pltpu.CompilerParams(vmem_limit_bytes=VMEM_LIMIT),
        name=name,
    )(*args)


def product(place, act, own, pieces, model):
    block, quarter = place[0], place[1]
    rows = own.shape[0]
    total = jnp.dot(
        act[:, pl.ds(pl.multiple_of(block * rows, rows), rows)], own[...], preferred_element_type=F32
    )
    for piece, (step, turn) in zip(pieces, model):
        part = piece.shape[0]
        start = (block ^ step) * rows + (quarter ^ turn) * part
        total += jnp.dot(
            act[:, pl.ds(pl.multiple_of(start, part), part)], piece[...], preferred_element_type=F32
        )
    return total


def partial_kernel(model, groups, place, *rest):
    number = sum(groups)
    acts, own, pieces, outs = rest[:number], rest[number], rest[number + 1 : -len(groups)], rest[-len(groups) :]
    acts = list(acts)
    for size, out in zip(groups, outs):
        row = 0
        for act in acts[:size]:
            out[row : row + act.shape[0], :] = product(place, act, own, pieces, model).astype(out.dtype)
            row += act.shape[0]
        del acts[:size]


def pack_raw(raw, out):
    heads, tokens = raw.shape
    width = out.shape[1]
    row = tokens
    for first in range(0, tokens, width):
        value = raw[:, first : first + width]
        high = value.astype(BF16)
        out[row : row + heads, :] = high
        out[row + heads : row + 2 * heads, :] = (value - high.astype(F32)).astype(BF16)
        row += 2 * heads


def unpack_raw(packed, tokens, heads):
    width = packed.shape[1]
    parts = []
    row = tokens
    for _ in range(0, tokens, width):
        parts.append(packed[row : row + heads, :].astype(F32) + packed[row + heads : row + 2 * heads, :].astype(F32))
        row += 2 * heads
    return jnp.concatenate(parts, axis=1)


def extra_kernel(model, step_model, place, act_own, act_low, act_high, own, *rest):
    n = len(model)
    pieces = rest[:n]
    step_pieces = rest[n : n + len(step_model)]
    full, raw, packed = rest[-3:]
    first = 0
    for act in (act_own, act_low, act_high):
        here = slice(first, first + act.shape[0])
        first += act.shape[0]
        value = product(place, act, own, pieces, model)
        full[here, :] = value
        packed[here, :] = value.astype(BF16)
        total = None
        for piece, step in zip(step_pieces, step_model):
            rows = piece.shape[1]
            start = pl.multiple_of((place[0] ^ step) * rows, rows)
            part = lax.dot_general(piece[...], act[:, pl.ds(start, rows)], NT, preferred_element_type=F32)
            total = part if total is None else total + part
        raw[:, here] = total
    pack_raw(raw[...], packed)


def combine_kernel(full, raw, came, out):
    heads, tokens = raw.shape
    half = tokens // 2
    for a, b in ((0, half), (half, 0)):
        out[a : a + half, :] = (full[a : a + half, :] + came[b : b + half, :].astype(F32)).astype(BF16)
    other = unpack_raw(came, tokens, heads)
    pack_raw(raw[...] + jnp.concatenate([other[:, half:], other[:, :half]], axis=1), out)


def decay_kernel(offsets, tokens, place, rate, *rest):
    packed = rest[:-4]
    factor, log_row, log_col, gain_col = rest[-4:]
    mine = place[2]
    heads = rate.shape[0]
    pairs = [unpack_raw(p, 2 * tokens, heads) for p in packed]
    lane = lax.broadcasted_iota(jnp.int32, (heads, tokens), 1)
    steps, logs, totals = [], [], []
    for at in range(len(offsets)):
        value = pairs[at // 2][:, at % 2 * tokens : (at % 2 + 1) * tokens]
        step = jnp.maximum(value, 0.0) + jnp.log1p(jnp.exp(-jnp.abs(value)))
        log = step * (-LOG2E * rate[...])
        shift = 1
        while shift < tokens:
            log = log + jnp.where(lane >= shift, pltpu.roll(log, shift, 1), 0.0)
            shift *= 2
        steps.append(step)
        logs.append(log)
        totals.append(log[:, tokens - 1 :])
    for at, offset in enumerate(offsets):
        here = slice(at * tokens, (at + 1) * tokens)
        if at == 0:
            factor[:, here] = steps[0]
            continue
        between = jnp.zeros_like(totals[0])
        first = mine ^ offset
        for other, distance in enumerate(offsets):
            block = mine ^ distance
            inside = jnp.logical_and(block > first, block < mine)
            between += jnp.where(inside, totals[other], 0.0)
        factor[:, here] = steps[at] * jnp.exp2(totals[at] - logs[at] + between)
    log_row[...] = logs[0]
    wide = jnp.concatenate([logs[0], jnp.zeros((128 - heads, tokens), F32)], axis=0)
    turned = wide.T
    log_col[...] = turned
    gain_col[...] = jnp.exp2(turned)


def causal_of(tokens):
    row = lax.broadcasted_iota(jnp.int32, (tokens, tokens), 0)
    col = lax.broadcasted_iota(jnp.int32, (tokens, tokens), 1)
    return col <= row


def folded(combine, value):
    parts = [value[:, i : i + 128] for i in range(0, value.shape[1], 128)]
    return functools.reduce(combine, parts)


SCALE = LOG2E * HEAD_DIM ** -0.5


def for_place(mine, offsets, body):
    for position in range(len(offsets)):
        earlier = [at for at in range(1, len(offsets)) if (position ^ offsets[at]) < position]
        pl.when(mine == position)(functools.partial(body, earlier))


def teacher_kernel(offsets, place, query, *rest):
    keys, norm = rest[:-1], rest[-1]
    tokens = query.shape[0]

    def body(earlier):
        asked = query[...]
        scores = []
        for at in [0] + earlier:
            key = keys[at // 2][pl.ds(at % 2 * tokens, tokens), :]
            scores.append(lax.dot_general(asked, key, NT, preferred_element_type=F32) * SCALE)
        scores[0] = jnp.where(causal_of(tokens), scores[0], -jnp.inf)
        top = functools.reduce(jnp.maximum, [folded(jnp.maximum, s) for s in scores])
        peak = jnp.max(top, axis=1, keepdims=True)
        mass = functools.reduce(jnp.add, [folded(jnp.add, jnp.exp2(s - peak)) for s in scores])
        total = jnp.sum(mass, axis=1, keepdims=True)
        norm[0] = jnp.broadcast_to(peak + jnp.log2(total), (tokens, 128))

    for_place(place[2], offsets, body)


def loss_kernel(
    offsets, first, heads, number, place, query, kept, norm, factor, log_row, log_col, gain_col, *rest
):
    arrived, rest, out = rest[:number], rest[number:-1], rest[-1]
    keys, inputs = rest[: len(rest) // 2], rest[len(rest) // 2 :]
    tokens = query.shape[0]

    lane = lax.broadcasted_iota(jnp.int32, (tokens, 128), 1)

    def body(earlier):
        def one_head(i, carry):
            head = first + i
            cols = pl.ds(pl.multiple_of(i * HEAD_DIM, HEAD_DIM), HEAD_DIM)

            def column(ref):
                return jnp.sum(jnp.where(lane == head, ref[...], 0.0), axis=1, keepdims=True)

            asked = query[:, cols]
            came = jnp.concatenate([a[:, cols] for a in arrived], axis=0)
            read = (kept[:, cols] + came.astype(F32)).astype(BF16)
            lse = jnp.concatenate([norm[i]] * (tokens // 128), axis=1)
            gain = column(gain_col)
            sums = None
            for at in [0] + earlier:
                rows = pl.ds(at % 2 * tokens, tokens)
                score = lax.dot_general(asked, keys[at // 2][rows, :], NT, preferred_element_type=F32) * SCALE
                inner = lax.dot_general(read, inputs[at // 2][rows, :], NT, preferred_element_type=F32)
                inner = inner * factor[pl.ds(head, 1), at * tokens : (at + 1) * tokens]
                prob = jnp.exp2(score - lse)
                if at == 0:
                    gap = column(log_col) - log_row[pl.ds(head, 1), :]
                    diff = jnp.where(causal_of(tokens), prob - inner * jnp.exp2(gap), 0.0)
                else:
                    diff = prob - inner * gain
                square = folded(jnp.add, diff * diff)
                sums = square if sums is None else sums + square
            out[i] = jnp.sum(sums.T, axis=0, keepdims=True)
            return carry

        lax.fori_loop(0, heads, one_head, 0, unroll=2 if heads % 2 == 0 else 1)

    for_place(place[2], offsets, body)


class Order:
    def __init__(self):
        self.last = ()

    def gate(self, value):
        if not self.last:
            return value
        value, self.last = lax.optimization_barrier((value, self.last))
        return value

    def wait(self, value):
        value, _ = lax.optimization_barrier((value, self.last))
        self.last = tuple(jax.tree.leaves(value))
        return value


def xor_sums(offset_size, scale):
    got = [0]
    d = 1
    while d < offset_size:
        got += [g ^ (d * scale) for g in got]
        d *= 2
    return got


def spread(pieces, axis):
    got = list(pieces)
    d = 1
    while d < lax.axis_size(axis):
        got += [xor_permute(g, axis, d) for g in got]
        d *= 2
    return got


def local(hidden_in, teacher_query, teacher_key, proj_c, proj_b, proj_step, decay_rate):
    _, tokens, _ = hidden_in.shape
    hidden = hidden_in[0]
    rows, width = proj_c.shape
    head_count = proj_step.shape[1]
    seq, sides = lax.axis_size("seq"), lax.axis_size("head")
    half = seq // 2
    copies_y, copies_c = lax.axis_size("groups"), lax.axis_size("batch")
    copies = copies_y * copies_c
    z, x = lax.axis_index("seq"), lax.axis_index("head")
    side = z // half
    quarter = lax.axis_index("groups") * copies_c + lax.axis_index("batch")
    place = jnp.stack([z % half, quarter, z]).astype(jnp.int32)
    per_model_group = HEADS // KV_HEADS
    group_count = max(1, head_count // per_model_group)
    per_group = head_count // group_count
    group_first = x * head_count // per_model_group
    width_b = group_count * HEAD_DIM
    offsets = [0, half]
    for d in range(1, half):
        offsets += [d, d ^ half]
    padded = max(16, head_count)
    span = seq * tokens
    chunk = max(HEAD_DIM, width // 4)
    count = width // chunk
    heads = chunk // HEAD_DIM
    part = rows // copies
    turns = xor_sums(copies_y, copies_c)
    turns = [t ^ c for c in xor_sums(copies_c, 1) for t in turns]
    model = [(d, t) for d in range(1, half) for t in turns]
    query = teacher_query[0]
    order = Order()

    def over_half(value):
        return [xor_permute(value, "seq", d) for d in range(1, half)]

    def start_weights(first, last):
        piece = lax.dynamic_slice(proj_c, (quarter * part, first * chunk), (part, (last - first) * chunk))
        if first == 0:
            extra = lax.dynamic_slice(proj_b, (quarter * part, group_first * HEAD_DIM), (part, width_b))
            piece = jnp.concatenate([piece, extra], axis=1)
        return over_half(piece)

    def send(value):
        return xor_permute(value, "seq", half)

    def partial(acts, j):
        first, _, pieces = next(w for w in weights if w[0] <= j < w[1])
        flat_acts = [a for blocks, _ in acts for a in blocks]
        return order.wait(
            call(
                functools.partial(partial_kernel, model, [len(blocks) for blocks, _ in acts]),
                (order.gate(place), *flat_acts, proj_c, *pieces),
                [smem()]
                + [whole(a.shape) for a in flat_acts]
                + [columns(rows, chunk, j)]
                + [columns(part, chunk, j - first)] * len(model),
                [jax.ShapeDtypeStruct((sum(a.shape[0] for a in blocks), chunk), dtype) for blocks, dtype in acts],
                "partial",
            )
        )

    def teacher(first, number):
        return pl.pallas_call(
            functools.partial(teacher_kernel, offsets),
            grid=(number,),
            in_specs=[
                smem(),
                pl.BlockSpec((tokens, HEAD_DIM), lambda h: (0, first + h)),
            ]
            + [pl.BlockSpec((2 * tokens, HEAD_DIM), lambda h: (0, (first + h) // per_group))] * half,
            out_specs=pl.BlockSpec((1, tokens, 128), lambda h: (h, 0, 0)),
            out_shape=jax.ShapeDtypeStruct((number, tokens, 128), F32),
            compiler_params=pltpu.CompilerParams(vmem_limit_bytes=VMEM_LIMIT),
            name="teacher",
        )(order.gate(place), query, *keys)

    spans = [(0, 1), (1, 2), (2, 4)]
    weights = []
    local_key = lax.dynamic_slice_in_dim(teacher_key[0], group_first * HEAD_DIM, width_b, 1)
    local_b = lax.dynamic_slice_in_dim(proj_b, group_first * HEAD_DIM, width_b, 1)
    step_t = jnp.pad(proj_step.T, ((0, padded - head_count), (0, 0)))

    if sides == 2:
        cut = tokens // 4
        spots = [(i, j) for i in range(seq) for j in range(2)]
        flat = lambda i, j: i * 2 + j
        both = ("seq", "head")
        level = side == x
        even = [s for s in spots if s[0] // half == s[1]]
        odd = [s for s in spots if s[0] // half != s[1]]
        over = lambda value, group: lax.ppermute(value, both, [(flat(i, j), flat(i ^ half, j)) for i, j in group])
        row = [hidden[i * cut : (i + 1) * cut] for i in range(4)]
        across = lambda value: lax.ppermute(value, both, [(flat(i, j), flat(i, 1 - j)) for i, j in even])
        direct = [over(row[0], odd), over(row[2], odd)]
        swapped = [xor_permute(row[1], "head", 1), xor_permute(row[3], "head", 1)]
        key_half = xor_permute(local_key, "seq", half)
        w0 = start_weights(0, 1)
        w1 = start_weights(1, 2)
        w2 = start_weights(2, 4)
        step_rest = over_half(step_t)
        swapped[0] = order.wait(swapped[0])
        relayed = [over(swapped[0], even), None]
        swapped[1] = order.wait(swapped[1])
        relayed[1] = over(swapped[1], even)
        moved = [across(order.gate(row[0])), None]
        w0 = spread(order.wait(w0), "groups")

        def swap(i):
            got = order.wait((direct[i], relayed[i]))
            first = jnp.where(level, got[0], got[1])
            return first, xor_permute(first, "head", 1)

        def join(first, second):
            second = order.wait(second)
            return jnp.concatenate([jnp.where(level, first, second), jnp.where(level, second, first)], axis=0)

        first0, second0 = swap(0)
        moved[0] = order.wait(moved[0])
        moved[1] = across(order.gate(row[2]))
        w0 = spread(order.wait(w0), "batch")
        w1 = spread(order.wait(w1), "groups")
        others = [join(first0, second0)]
        weights.append((0, 1, order.wait(w0)))
        first1, second1 = swap(1)
        moved[1] = order.wait(moved[1])
        w1 = spread(order.wait(w1), "batch")
        mine = order.wait(
            jnp.where(level, hidden, jnp.concatenate([moved[0], swapped[0], moved[1], swapped[1]], axis=0))
        )
        key_half = order.wait(key_half)
        key_pair = jnp.concatenate([local_key, key_half], axis=0)
        key_rest = over_half(key_pair)
        step_rest = order.wait(step_rest)
        others.append(join(first1, second1))

    else:
        full = lax.all_gather(hidden, "head", axis=1, tiled=True)
        span_half = full.shape[1] // 2
        share = tokens // sides
        mine = lax.dynamic_slice_in_dim(full, side * span_half, span_half, 1)
        leaving = lax.dynamic_slice(full, (x * share, (1 - side) * span_half), (share, span_half))
        came = lax.all_gather(xor_permute(leaving, "seq", half), "head", axis=0, tiled=True)
        others = [came[: tokens // 2], came[tokens // 2 :]]
        key_pair = jnp.concatenate([local_key, xor_permute(local_key, "seq", half)], axis=0)
        step_rest = over_half(step_t)
        weights.append((0, 1, spread(spread(start_weights(0, 1), "groups"), "batch")))
        w1 = spread(spread(start_weights(1, 2), "groups"), "batch")
        w2 = start_weights(2, 4)
        key_rest = over_half(key_pair)

    packed_rows = 2 * tokens + 2 * padded * (2 * tokens // width_b)
    packed_shape = jax.ShapeDtypeStruct((packed_rows, width_b), BF16)
    extra_out = [
        jax.ShapeDtypeStruct((2 * tokens, width_b), F32),
        jax.ShapeDtypeStruct((padded, 2 * tokens), F32),
        packed_shape,
    ]
    acts = (mine, *others)
    full, raw, packed = order.wait(
        call(
            functools.partial(extra_kernel, model, list(range(half))),
            (order.gate(place), *acts, local_b, *weights[0][2], step_t, *step_rest),
            [smem()]
            + [whole(a.shape) for a in acts]
            + [whole(local_b.shape)]
            + [columns(part, width_b, chunk // width_b)] * len(model)
            + [whole(step_t.shape)] * half,
            extra_out,
            "extra",
        )
    )
    came = send(packed)
    w2 = spread(order.wait(w2), "groups")
    kept, arrived, norms = [], [], []
    def full_partial(j):
        leaving, stays = partial([(others, BF16), ([mine], F32)], j)
        arrived.append([send(leaving)])
        kept.append(stays)

    full_partial(0)
    weights.append((1, 2, order.wait(w1)))
    full_partial(1)
    key_rest = order.wait(key_rest)
    keys = [key_pair] + key_rest
    norms.append(order.wait(teacher(0, heads)))
    came = order.wait(came)
    pair = order.wait(
        call(
            combine_kernel,
            (full, raw, came),
            [whole(full.shape), whole(raw.shape), whole(came.shape)],
            [packed_shape],
            "combine",
        )[0]
    )
    pair_rest = over_half(pair)
    norms.append(order.wait(teacher(heads, heads)))
    arrived[0] = order.wait(arrived[0])
    w2 = spread(order.wait(w2), "batch")
    weights.append((2, 4, order.wait(w2)))
    full_partial(2)
    norms.append(order.wait(teacher(2 * heads, heads)))
    arrived[1] = order.wait(arrived[1])
    full_partial(3)
    norms.append(order.wait(teacher(3 * heads, heads)))
    inputs = [pair] + order.wait(pair_rest)
    rate = jnp.pad(decay_rate, (0, padded - head_count))[:, None]
    factor, log_row, log_col, gain_col = call(
        functools.partial(decay_kernel, offsets, tokens),
        (order.gate(place), rate, *inputs),
        [smem(), whole(rate.shape)] + [whole(packed_shape.shape)] * half,
        [
            jax.ShapeDtypeStruct((padded, span), F32),
            jax.ShapeDtypeStruct((padded, tokens), F32),
            jax.ShapeDtypeStruct((tokens, 128), F32),
            jax.ShapeDtypeStruct((tokens, 128), F32),
        ],
        "decay",
    )
    factor = order.wait(factor)

    losses = []
    for j in range(count):
        group = j * heads // per_group
        came = order.wait(arrived[j])
        losses.append(
            order.wait(
                call(
                    functools.partial(loss_kernel, offsets, j * heads, heads, len(came)),
                    (place, query, kept[j], norms[j], factor, log_row, log_col, gain_col, *came, *keys, *inputs),
                    [
                        smem(),
                        columns(tokens, chunk, j),
                        whole((tokens, chunk)),
                        whole(norms[j].shape),
                        whole(factor.shape),
                        whole(log_row.shape),
                        whole(log_col.shape),
                        whole(gain_col.shape),
                    ]
                    + [whole(c.shape) for c in came]
                    + [columns(2 * tokens, HEAD_DIM, group)] * (2 * half),
                    [jax.ShapeDtypeStruct((heads, 1, tokens), F32)],
                    "loss",
                )[0]
            )
        )
    return jnp.concatenate(losses, axis=0).reshape(1, head_count, tokens)


def solution(mesh):
    in_specs = (
        P(("groups", "batch"), "seq", "head"),
        P(("groups", "batch"), "seq", "head"),
        P(("groups", "batch"), "seq", None),
        P("seq", "head"),
        P("seq", None),
        P("seq", "head"),
        P("head"),
    )
    out_specs = P(("groups", "batch"), "head", "seq")
    return jax.shard_map(local, mesh=mesh, in_specs=in_specs, out_specs=out_specs, check_vma=False)
```
